32 devices in a mesh: group: 2 (over y), tm: 4 (over x, core), inst: 4 (over z).
Axes of the slice: x: 2, y: 2, z: 4, core: 2. Of those that a mesh axis runs over, the one named last changes fastest.
Arguments:
- quotes: float32 [8, 16384], P(('group', 'tm'), 'inst'), parts along dimension 0, may hold values from -6 to 6
- present: int32 [8, 16384], P(('group', 'tm'), 'inst'), parts along dimension 0, may hold values from 0 to 1
- loadings: bfloat16 [16384, 512], P('inst'), may hold values from -0.07 to 0.07
- noise_var: float32 [16384], P('inst'), may hold values from 0.5 to 4
- persistence: float32 [512], replicated, may hold values from 0.2 to 0.99
- shock_var: float32 [512], replicated, may hold values from 0.05 to 0.5
Outputs:
- filtered_mean: float32 [8, 512], P(('group', 'tm')), parts along dimension 0
- filtered_var: float32 [8, 512], P(('group', 'tm')), parts along dimension 0
- smoothed_mean: float32 [8, 512], P(('group', 'tm')), parts along dimension 0
The draws below stay inside these ranges and needn't reach their ends.
There are 2 independent parts, one for each index of `group`. The reference program is written for one: setup_inputs(seed, part) draws one part's arguments, and reference() takes and returns one part's arrays. A program takes and returns all parts, laid end to end along the dimension named above; an argument that names none is the same for every part. Nothing has to cross between parts.
All inputs are finite; a program needn't handle non-finite values.
Results may differ from the reference program's by a relative error of at most 0.0027.
Values sent between devices are 32-bit elements; how exact they have to be, the bound alone decides.
A program may use at most 128 MiB of HBM per device.

```python
import math
import jax
import jax.numpy as jnp
from jax import lax

FACTORS = 512
INST = 16384
STEPS = 4


sector_count = 16


def draw_present(key, part):
    on_key = jax.random.fold_in(key, 101)
    inside_key = jax.random.fold_in(key, 102)
    sector_on = jax.random.randint(on_key, (STEPS, sector_count), 0, 2)
    inside = (jax.random.randint(inside_key, (STEPS, INST), 0, 8) < 7).astype(jnp.int32)
    sector_of = jnp.arange(INST) % sector_count
    return (sector_on[:, sector_of] * inside).astype(jnp.int32)


def draw_loadings(key, part):
    idio_key = jax.random.fold_in(key, 201)
    strength_key = jax.random.fold_in(key, 202)
    vector_key = jax.random.fold_in(key, 203)
    idio = jnp.clip(jax.random.normal(idio_key, (INST, FACTORS), jnp.float32), -4.0, 4.0)
    strength = jnp.clip(jax.random.normal(strength_key, (INST,), jnp.float32), -4.0, 4.0)
    vectors = jnp.clip(jax.random.normal(vector_key, (sector_count, FACTORS), jnp.float32), -4.0, 4.0)
    sector_of = jnp.arange(INST) % sector_count
    common = strength[:, None] * vectors[sector_of]
    values = (0.3 * idio + 2.0 * common) * (1.0 / math.sqrt(INST))
    return jnp.clip(values, -0.07, 0.07).astype(jnp.bfloat16)


def shard_levels(stream_key, extent, shards, least, high):
    gain, own = 1.0, jax.random.fold_in(stream_key, 6)
    for axis_at, blocks in shards:
        heights = jnp.exp(jax.random.uniform(jax.random.fold_in(own, axis_at), (blocks,), jnp.float32, least / len(shards), high / len(shards)))
        gain = gain * jnp.repeat(heights, extent[axis_at] // blocks).reshape([-1 if axis == axis_at else 1 for axis in range(len(extent))])
    return gain


def scatter_about(own_key, dims, scale, most, pieces=(), held_as=jnp.bfloat16):
    entries = jax.random.normal(own_key, dims, jnp.float32) * scale
    if len(pieces) > 0:
        entries = shard_levels(own_key, dims, pieces, -0.22, 0.18) * entries
    return jnp.clip(entries, min=-most, max=most).astype(held_as)


def setup_inputs(seed: int = 0, part: int = 0) -> dict:
    key_of = jax.random.split(jax.random.key(seed), 7)
    own_keys = jax.random.split(jax.random.fold_in(key_of[6], part), 7)
    return {
        "quotes": scatter_about(own_keys[0], (STEPS, INST), 1.0, 6.0, ((0, 4), (1, 4)), jnp.float32),
        "present": draw_present(jax.random.fold_in(jax.random.fold_in(key_of[6], part), 71), part),
        "loadings": draw_loadings(jax.random.fold_in(key_of[6], 71), part),
        "noise_var": jnp.clip(jnp.exp(math.log(4.0) - 2.0794415 * jax.random.uniform(key_of[3], (INST,), jnp.float32) ** shard_levels(key_of[3], (INST,), ((0, 4),), -0.2, 0.2)), 0.5, 4.0),
        "persistence": jnp.clip(jax.random.uniform(key_of[4], (FACTORS,), jnp.float32, 0.2, 0.99), 0.2, 0.99),
        "shock_var": jnp.clip(jnp.exp(jax.random.uniform(key_of[5], (FACTORS,), jnp.float32, math.log(0.05), math.log(0.5))), 0.05, 0.5),
    }


highest = lax.Precision.HIGHEST

def step_information(loadings, noise_var, row_quotes, row_present):
    scaled = row_present.astype(jnp.float32) / noise_var
    weighted = (loadings.astype(jnp.float32) * scaled[:, None]).astype(jnp.bfloat16)
    info_matrix = lax.dot_general(weighted.astype(jnp.float32), loadings.astype(jnp.float32), (((0,), (0,)), ((), ())), preferred_element_type=jnp.float32)
    info_vector = jnp.dot(row_quotes, weighted.astype(jnp.float32), precision=highest)
    return (info_matrix, info_vector)

def reference(quotes, present, loadings, noise_var, persistence, shock_var):
    factors = loadings.shape[1]
    identity_matrix = jnp.eye(factors, dtype=jnp.float32)

    def gather_step(inputs):
        return step_information(loadings, noise_var, inputs[0], inputs[1])
    info_matrix, info_vector = lax.map(gather_step, (quotes, present))

    def forward(carried_state, inputs):
        prior_mean, prior_cov = carried_state
        pred_mean = persistence * prior_mean
        pred_cov = persistence[:, None] * prior_cov * persistence[None, :] + jnp.diag(shock_var)
        pred_prec = jnp.linalg.solve(pred_cov, identity_matrix)
        post_cov = jnp.linalg.solve(pred_prec + inputs[0], identity_matrix)
        post_mean = jnp.dot(post_cov, jnp.dot(pred_prec, pred_mean, precision=highest) + inputs[1], precision=highest)
        return ((post_mean, post_cov), (post_mean, post_cov))
    initial = (jnp.zeros((factors,), jnp.float32), jnp.zeros((factors, factors), jnp.float32))
    _, (means, covs) = lax.scan(forward, initial, (info_matrix, info_vector))

    def backward(next_value, inputs):
        mean_now, cov_now = inputs
        pred_cov = persistence[:, None] * cov_now * persistence[None, :] + jnp.diag(shock_var)
        smoother_gain = jnp.linalg.solve(pred_cov, persistence[:, None] * cov_now.T).T
        smoothed = mean_now + jnp.dot(smoother_gain, next_value - persistence * mean_now, precision=highest)
        return (smoothed, smoothed)
    _, earlier_values = lax.scan(backward, means[-1], (means[:-1], covs[:-1]), reverse=True)
    smoothed_mean = jnp.concatenate([earlier_values, means[-1:]], axis=0)
    filtered_var = jnp.diagonal(covs, axis1=1, axis2=2)
    return (means, filtered_var, smoothed_mean)
```

```python
import functools

import jax
import jax.numpy as jnp
from jax import lax
from jax.experimental import pallas as pl
from jax.experimental.pallas import tpu as pltpu
from jax.sharding import PartitionSpec as P

f32 = jnp.float32
bf16 = jnp.bfloat16
highest = lax.Precision.HIGHEST


def mm(left, right):
    return jnp.dot(left, right, preferred_element_type=f32)


def mm_full(left, right):
    return jnp.dot(left, right, precision=highest, preferred_element_type=f32)


def eye_mask(size):
    rows = lax.broadcasted_iota(jnp.int32, (size, size), 0)
    columns = lax.broadcasted_iota(jnp.int32, (size, size), 1)
    return rows == columns


def total(matrix):
    return jnp.sum(jnp.sum(matrix, axis=0, keepdims=True), axis=1, keepdims=True)


def to_col(row, ident_ref):
    return jnp.sum(ident_ref[...] * row, axis=1, keepdims=True)


def row_times(matrix, row):
    return jnp.sum(matrix.astype(f32) * row, axis=1, keepdims=True)


def times_col(matrix, col):
    return jnp.sum(matrix.astype(f32) * col, axis=0, keepdims=True)


def slower(rate):
    return rate * rate / (2.0 - rate * rate)


def start(a_ref, ah_ref, x_ref, ident_ref):
    square = mm(ah_ref[...], ah_ref[...])
    fourth = total(square * square)
    upper = jnp.maximum(jnp.sqrt(jnp.sqrt(fourth)) * 1.01, 1.5)
    lower = 0.98
    slope = 2.0 / (upper - lower)
    centre = (upper + lower) / (upper - lower)
    height = 1.0 / ((4.0 * centre * centre - 3.0) * centre)
    c0 = (12.0 * centre * centre - 3.0) * slope * height
    c1 = -12.0 * centre * slope * slope * height
    c2 = 4.0 * slope * slope * slope * height
    x_ref[...] = (c0 * ident_ref[...] + c1 * a_ref[...] + c2 * square).astype(bf16)
    return upper, height


def newton(ah_ref, x_ref, e_ref, ident_ref, rate):
    weight = 2.0 / (2.0 - rate * rate)
    e_ref[...] = (ident_ref[...] - mm(ah_ref[...], x_ref[...])).astype(bf16)
    x_ref[...] = (weight * (x_ref[...].astype(f32) + mm(x_ref[...], e_ref[...]))).astype(bf16)
    return slower(rate)


def more_steps(rate):
    count = jnp.zeros_like(rate)
    for _ in range(10):
        count = count + jnp.where(rate > 0.045, 1.0, 0.0)
        rate = slower(rate)
    return jnp.max(count).astype(jnp.int32)


def finish(a_ref, ah_ref, x_ref, e_ref, out_ref, ident_ref):
    low = (a_ref[...] - ah_ref[...].astype(f32)).astype(bf16)
    e = ident_ref[...] - (mm(ah_ref[...], x_ref[...]) + mm(low, x_ref[...]))
    e_ref[...] = e.astype(bf16)
    twice = mm(e_ref[...], e_ref[...])
    e_ref[...] = (e + twice).astype(bf16)
    out_ref[...] = x_ref[...].astype(f32) + mm(x_ref[...], e_ref[...])
    return jnp.max(total(twice * twice))


def careful(a_ref, out_ref, work_ref, ident_ref, upper):
    out_ref[...] = (1.0 / upper) * ident_ref[...]

    def residual():
        e = ident_ref[...] - mm_full(a_ref[...], out_ref[...])
        work_ref[...] = e
        return jnp.sum(e * e)

    def more(state):
        return (state[1] > 1e-6) & (state[0] < 60)

    def refine(state):
        out_ref[...] = out_ref[...] + mm_full(out_ref[...], work_ref[...])
        return (state[0] + 1, residual())

    lax.while_loop(more, refine, (jnp.int32(0), residual()))


piece = 32
MESH = pl.DeviceIdType.MESH


def pieces_of(size):
    blocks = size // 128
    return [
        (row, column, part)
        for row in range(blocks)
        for column in range(row + 1)
        for part in range(128 // piece)
    ]


def spread_kernel(insts, times, g_ref, h_ref, all_ref, pack, landed, *sems):
    rs_send, rs_recv, z_send, z_recv, x_send, x_recv, s_send, s_recv = sems
    size = g_ref.shape[0]
    t, z = lax.axis_index("tm"), lax.axis_index("inst")
    pairs = times // 2
    spot, core = t // 2, t % 2
    sibling = t + 1 - 2 * core
    z_peers = [lax.rem(z + k, insts) for k in range(insts)]
    z_from = [lax.rem(z - k + insts, insts) for k in range(insts)]
    t_peers = [lax.rem(spot + j, pairs) * 2 + core for j in range(pairs)]
    t_from = [lax.rem(spot - j + pairs, pairs) * 2 + core for j in range(pairs)]

    barrier = pltpu.get_barrier_semaphore()
    others = [{"inst": p} for p in z_peers[1:]] + [{"tm": p} for p in t_peers[1:] + [sibling]]
    for other in others:
        pl.semaphore_signal(barrier, inc=1, device_id=other, device_id_type=MESH)

    places = pieces_of(size)
    per = len(places) // insts
    tail = per * piece
    for number, (row, column, part) in enumerate(places):
        pack[number // per, pl.ds((number % per) * piece, piece), :] = g_ref[
            pl.ds(row * 128 + part * piece, piece), pl.ds(column * 128, 128)
        ]
    for chunk in range(insts):
        pack[chunk, pl.ds(tail, 8), :] = jnp.zeros((8, 128), f32)
    for row in range(size // 128):
        pack[0, pl.ds(tail + row, 1), :] = h_ref[:, pl.ds(row * 128, 128)]
    pl.semaphore_wait(barrier, len(others))

    def remote(source, target, send, recv, device):
        return pltpu.make_async_remote_copy(
            src_ref=source, dst_ref=target, send_sem=send, recv_sem=recv,
            device_id=device, device_id_type=MESH,
        )

    sent = []

    def start(copy):
        copy.start()
        sent.append(copy)

    rs = [
        remote(pack.at[z_peers[k]], landed.at[k], rs_send.at[k], rs_recv.at[k], {"inst": z_peers[k]})
        for k in range(1, insts)
    ]
    for copy in rs:
        start(copy)
    for copy in rs:
        copy.wait_recv()
    total = pack[z]
    for k in range(1, insts):
        total = total + landed[k]
    all_ref[t, z] = total

    def along_z(k, chunk, peer):
        here = all_ref.at[t, chunk]
        return remote(here, here, z_send.at[k], z_recv.at[k], {"inst": peer})

    def along_x(j, q, step, chunk, peer):
        here = all_ref.at[step, chunk]
        return remote(here, here, x_send.at[j, q], x_recv.at[j, q], {"tm": peer})

    def to_sibling(j, q, step, chunk):
        here = all_ref.at[step, chunk]
        return remote(here, here, s_send.at[j, q], s_recv.at[j, q], {"tm": sibling})

    for k in range(1, insts):
        start(along_z(k, z, z_peers[k]))
    for q in range(insts + 1):
        if q < insts:
            chunk = z_from[q]
            if q > 0:
                along_z(q, chunk, z_peers[q]).wait_recv()
            for j in range(1, pairs):
                start(along_x(j, q, t, chunk, t_peers[j]))
            start(to_sibling(0, q, t, chunk))
        if q > 0:
            chunk = z_from[q - 1]
            for j in range(1, pairs):
                along_x(j, q - 1, t_from[j], chunk, t_peers[j]).wait_recv()
                start(to_sibling(j, q - 1, t_from[j], chunk))
    for q in range(insts):
        for j in range(pairs):
            source = t_from[j] + 1 - 2 * core
            to_sibling(j, q, source, z_from[q]).wait_recv()
    for copy in sent:
        copy.wait_send()


def spread(matrix, vector, insts, times):
    size = matrix.shape[0]
    rows = len(pieces_of(size)) // insts * piece + 8
    whole = pl.BlockSpec(memory_space=pltpu.VMEM)
    dma = pltpu.SemaphoreType.DMA
    pairs = times // 2
    return pl.pallas_call(
        functools.partial(spread_kernel, insts, times),
        out_shape=jax.ShapeDtypeStruct((times, insts, rows, 128), f32),
        in_specs=[whole, whole],
        out_specs=whole,
        scratch_shapes=[
            pltpu.VMEM((insts, rows, 128), f32), pltpu.VMEM((insts, rows, 128), f32),
            dma((insts,)), dma((insts,)), dma((insts,)), dma((insts,)),
            dma((pairs, insts)), dma((pairs, insts)), dma((pairs, insts)), dma((pairs, insts)),
        ],
        compiler_params=pltpu.CompilerParams(
            collective_id=0, has_side_effects=True, vmem_limit_bytes=48 * 1024 * 1024
        ),
    )(matrix, vector)


def unpack(g_ref, index, a_ref):
    size = a_ref.shape[0]
    places = pieces_of(size)
    per = len(places) // g_ref.shape[1]
    for number, (row, column, part) in enumerate(places):
        a_ref[pl.ds(row * 128 + part * piece, piece), pl.ds(column * 128, 128)] = g_ref[
            index, number // per, pl.ds((number % per) * piece, piece), :
        ]
    for row in range(size // 128):
        for column in range(row):
            below = a_ref[pl.ds(row * 128, 128), pl.ds(column * 128, 128)]
            a_ref[pl.ds(column * 128, 128), pl.ds(row * 128, 128)] = below.T
    rows = g_ref[index, 0, pl.ds(per * piece, 8), :]
    return jnp.concatenate([rows[row : row + 1] for row in range(size // 128)], axis=1)


def chain_kernel(
    own_ref, g_ref, frow_ref, qrow_ref,
    mean_ref, var_ref, smooth_ref,
    x_all, s_rows, s_cols, y_rows, own_y,
    g_full, a_ref, ah_ref, xh_ref, e_ref, own_a, own_ah, own_xh, own_e, own_x, own_row,
    work_ref, ident_ref,
):
    steps, size = g_ref.shape[0], frow_ref.shape[1]
    own = own_ref[0]
    ident_ref[...] = jnp.where(eye_mask(size), f32(1.0), f32(0.0))
    x_all[0] = jnp.zeros((size, size), f32)
    s_rows[0] = jnp.zeros((1, size), f32)
    s_cols[0] = jnp.zeros((size, 1), f32)
    y_rows[0] = jnp.zeros((1, size), f32)
    frow = frow_ref[...]
    fcol = to_col(frow, ident_ref)
    sq_row = jnp.sqrt(qrow_ref[...])
    sq_col = to_col(sq_row, ident_ref)
    f2_row, f2_col = frow * frow, fcol * fcol

    def build(index, prior_row, prior_col, extra):
        before = jnp.maximum(index - 1, 0)
        y = unpack(g_ref, index, g_full) * sq_row
        old_row, old_col = s_rows[before], s_cols[before]
        carried = times_col(x_all[before], old_col * to_col(y_rows[before], ident_ref))
        y = y + frow * (old_row * carried)

        def scaled(row, col, diagonal):
            kept = (fcol * old_col * col) * (frow * old_row * row)
            added = (sq_col * col) * (sq_row * row)
            inner = g_full[...] * added - x_all[before] * kept
            return inner + ident_ref[...] * (row * row * diagonal)

        row, col = lax.rsqrt(prior_row + extra * f2_row), lax.rsqrt(prior_col + extra * f2_col)
        a = scaled(row, col, 1.0 + extra * f2_row)
        a_ref[...] = a
        ah_ref[...] = a.astype(bf16)

        @pl.when(index == own)
        def _():
            row, col = lax.rsqrt(prior_row), lax.rsqrt(prior_col)
            a = scaled(row, col, f32(1.0))
            own_a[...] = a
            own_ah[...] = a.astype(bf16)
            own_row[...] = row
            own_y[...] = y

        y_rows[index] = y
        s_rows[index] = row
        s_cols[index] = col

    def step(index, carry):
        prior_row, prior_col = carry
        build(index, prior_row, prior_col, 1.0)
        upper, rate = start(a_ref, ah_ref, xh_ref, ident_ref)
        for _ in range(2):
            rate = newton(ah_ref, xh_ref, e_ref, ident_ref, rate)
        lax.fori_loop(
            0, more_steps(rate), lambda _, r: newton(ah_ref, xh_ref, e_ref, ident_ref, r), rate
        )
        off = finish(a_ref, ah_ref, xh_ref, e_ref, x_all.at[index], ident_ref)

        @pl.when(jnp.logical_not(off < 0.002))
        def _():
            careful(a_ref, x_all.at[index], work_ref, ident_ref, upper)

        return prior_row / (prior_row + f2_row), prior_col / (prior_col + f2_col)

    ones = (jnp.ones((1, size), f32), jnp.ones((size, 1), f32))
    prior_row, prior_col = lax.fori_loop(0, steps - 1, step, ones)
    build(steps - 1, prior_row, prior_col, 0.0)
    upper, rate = start(a_ref, ah_ref, xh_ref, ident_ref)
    own_upper, own_rate = start(own_a, own_ah, own_xh, ident_ref)

    def both(_, rates):
        return (
            newton(ah_ref, xh_ref, e_ref, ident_ref, rates[0]),
            newton(own_ah, own_xh, own_e, ident_ref, rates[1]),
        )

    rates = (rate, own_rate)
    for _ in range(3):
        rates = both(0, rates)
    lax.fori_loop(0, jnp.maximum(more_steps(rates[0]), more_steps(rates[1])), both, rates)
    own_off = finish(own_a, own_ah, own_xh, own_e, own_x, ident_ref)

    @pl.when(jnp.logical_not(own_off < 0.002))
    def _():
        careful(own_a, own_x, work_ref, ident_ref, own_upper)

    own_scale = own_row[...]
    mean_ref[...] = sq_row * own_scale * times_col(own_x[...], to_col(own_scale * own_y[...], ident_ref))
    diagonal = jnp.sum(ident_ref[...] * own_x[...], axis=0, keepdims=True)
    var_ref[...] = qrow_ref[...] * own_scale * own_scale * diagonal

    last_row = s_rows[steps - 1]
    goal = last_row * y_rows[steps - 1]
    x = row_times(xh_ref[...], goal)
    for _ in range(2):
        x = x + row_times(xh_ref[...], goal - times_col(a_ref[...], x))
    rest = goal - times_col(a_ref[...], x)
    y_rows[steps - 1] = last_row * jnp.sum(ident_ref[...] * x, axis=0, keepdims=True)
    missed = jnp.max(total(rest * rest) - 2e-7 * total(x * x))

    @pl.when(jnp.logical_not(missed <= 0.0))
    def _():
        careful(a_ref, own_x, work_ref, ident_ref, upper)
        y_rows[steps - 1] = last_row * times_col(own_x[...], to_col(goal, ident_ref))

    def back(count, later):
        index = steps - 2 - count
        value = s_rows[index] * (y_rows[index] + frow * later)
        return s_rows[index] * times_col(x_all[index], to_col(value, ident_ref))

    smooth_ref[...] = sq_row * lax.fori_loop(0, steps - 1 - own, back, y_rows[steps - 1])


def chain(own, matrices, persistence, shock_var):
    steps, size = matrices.shape[0], persistence.shape[0]
    row = jax.ShapeDtypeStruct((1, size), f32)
    square = pltpu.VMEM((size, size), f32)
    half = pltpu.VMEM((size, size), bf16)
    flat = pltpu.VMEM((1, size), f32)
    whole = pl.BlockSpec(memory_space=pltpu.VMEM)
    return pl.pallas_call(
        chain_kernel,
        out_shape=(row, row, row),
        in_specs=[pl.BlockSpec(memory_space=pltpu.SMEM)] + [whole] * 3,
        out_specs=(whole, whole, whole),
        scratch_shapes=[
            pltpu.VMEM((steps, size, size), f32), pltpu.VMEM((steps, 1, size), f32),
            pltpu.VMEM((steps, size, 1), f32), pltpu.VMEM((steps, 1, size), f32), flat,
            square, square, half, half, half, square, half, half, half, square, flat,
            square, square,
        ],
        compiler_params=pltpu.CompilerParams(vmem_limit_bytes=60 * 1024 * 1024),
    )(
        own, matrices, persistence[None, :], shock_var[None, :],
    )


def information_kernel(quotes_ref, present_ref, noise_ref, loadings_ref, matrix_ref, vector_ref):
    @pl.when(pl.program_id(0) == 0)
    def _():
        matrix_ref[...] = jnp.zeros_like(matrix_ref)
        vector_ref[...] = jnp.zeros_like(vector_ref)

    loadings = loadings_ref[...]
    scaled = present_ref[...].astype(f32) / noise_ref[...]
    weighted = (loadings.T.astype(f32) * scaled).astype(bf16)
    matrix_ref[...] += mm(weighted, loadings)
    quotes = quotes_ref[...]
    high = quotes.astype(bf16).astype(f32)
    rest = quotes - high
    middle = rest.astype(bf16).astype(f32)
    index = lax.broadcasted_iota(jnp.int32, (16, quotes.shape[1]), 0)
    rows = jnp.where(index == 0, high, jnp.where(index == 1, middle, 0.0))
    rows = jnp.where(index == 2, rest - middle, rows).astype(bf16)
    sums = lax.dot_general(rows, weighted, (((1,), (1,)), ((), ())), preferred_element_type=f32)
    vector_ref[...] += jnp.sum(sums, axis=0, keepdims=True)


def step_information(loadings, noise_var, quotes, present):
    insts, size = loadings.shape
    chunk = 1024 if insts % 1024 == 0 else 512
    flat = pl.BlockSpec((1, chunk), lambda i: (0, i))
    return pl.pallas_call(
        information_kernel,
        grid=(insts // chunk,),
        out_shape=(
            jax.ShapeDtypeStruct((size, size), f32), jax.ShapeDtypeStruct((1, size), f32),
        ),
        in_specs=[flat, flat, flat, pl.BlockSpec((chunk, size), lambda i: (i, 0))],
        out_specs=(
            pl.BlockSpec((size, size), lambda i: (0, 0)), pl.BlockSpec((1, size), lambda i: (0, 0)),
        ),
        compiler_params=pltpu.CompilerParams(vmem_limit_bytes=60 * 1024 * 1024),
    )(quotes, present, noise_var[None, :], loadings)


def body(quotes, present, loadings, noise_var, persistence, shock_var):
    parts = step_information(loadings, noise_var, quotes, present)
    matrices = spread(*parts, lax.axis_size("inst"), lax.axis_size("tm"))
    own = lax.axis_index("tm").astype(jnp.int32)[None]
    return chain(own, matrices, persistence, shock_var)


def solution(mesh):
    placed = (
        P(("group", "tm"), "inst"),
        P(("group", "tm"), "inst"),
        P("inst", None),
        P("inst"),
        P(),
        P(),
    )
    return jax.shard_map(
        body,
        mesh=mesh,
        in_specs=placed,
        out_specs=(P(("group", "tm"), None), P(("group", "tm"), None), P(("group", "tm"), None)),
        check_vma=False,
    )
```

```python
import functools

import jax
import jax.numpy as jnp
from jax import lax
from jax.experimental import pallas as pl
from jax.experimental.pallas import tpu as pltpu
from jax.sharding import PartitionSpec as P

f32 = jnp.float32
bf16 = jnp.bfloat16
highest = lax.Precision.HIGHEST


def mm(left, right):
    return jnp.dot(left, right, preferred_element_type=f32)


def mm_full(left, right):
    return jnp.dot(left, right, precision=highest, preferred_element_type=f32)


def eye_mask(size):
    rows = lax.broadcasted_iota(jnp.int32, (size, size), 0)
    columns = lax.broadcasted_iota(jnp.int32, (size, size), 1)
    return rows == columns


def total(matrix):
    return jnp.sum(jnp.sum(matrix, axis=0, keepdims=True), axis=1, keepdims=True)


def to_col(row, ident_ref):
    return jnp.sum(ident_ref[...] * row, axis=1, keepdims=True)


def row_times(matrix, row):
    return jnp.sum(matrix.astype(f32) * row, axis=1, keepdims=True)


def times_col(matrix, col):
    return jnp.sum(matrix.astype(f32) * col, axis=0, keepdims=True)


def slower(rate):
    return rate * rate / (2.0 - rate * rate)


def start(a_ref, ah_ref, x_ref, ident_ref):
    square = mm(ah_ref[...], ah_ref[...])
    fourth = total(square * square)
    upper = jnp.maximum(jnp.sqrt(jnp.sqrt(fourth)) * 1.01, 1.5)
    lower = 0.98
    slope = 2.0 / (upper - lower)
    centre = (upper + lower) / (upper - lower)
    height = 1.0 / ((4.0 * centre * centre - 3.0) * centre)
    c0 = (12.0 * centre * centre - 3.0) * slope * height
    c1 = -12.0 * centre * slope * slope * height
    c2 = 4.0 * slope * slope * slope * height
    x_ref[...] = (c0 * ident_ref[...] + c1 * a_ref[...] + c2 * square).astype(bf16)
    return upper, height


def newton(ah_ref, x_ref, e_ref, ident_ref, rate):
    weight = 2.0 / (2.0 - rate * rate)
    e_ref[...] = (ident_ref[...] - mm(ah_ref[...], x_ref[...])).astype(bf16)
    x_ref[...] = (weight * (x_ref[...].astype(f32) + mm(x_ref[...], e_ref[...]))).astype(bf16)
    return slower(rate)


def more_steps(rate):
    count = jnp.zeros_like(rate)
    for _ in range(10):
        count = count + jnp.where(rate > 0.045, 1.0, 0.0)
        rate = slower(rate)
    return jnp.max(count).astype(jnp.int32)


def finish(a_ref, ah_ref, x_ref, e_ref, out_ref, ident_ref):
    low = (a_ref[...] - ah_ref[...].astype(f32)).astype(bf16)
    e = ident_ref[...] - (mm(ah_ref[...], x_ref[...]) + mm(low, x_ref[...]))
    e_ref[...] = e.astype(bf16)
    twice = mm(e_ref[...], e_ref[...])
    e_ref[...] = (e + twice).astype(bf16)
    out_ref[...] = x_ref[...].astype(f32) + mm(x_ref[...], e_ref[...])
    return total(twice * twice)


def careful(a_ref, out_ref, work_ref, ident_ref, upper):
    out_ref[...] = (1.0 / upper) * ident_ref[...]

    def residual():
        e = ident_ref[...] - mm_full(a_ref[...], out_ref[...])
        work_ref[...] = e
        return jnp.sum(e * e)

    def more(state):
        return (state[1] > 1e-6) & (state[0] < 60)

    def refine(state):
        out_ref[...] = out_ref[...] + mm_full(out_ref[...], work_ref[...])
        return (state[0] + 1, residual())

    lax.while_loop(more, refine, (jnp.int32(0), residual()))


MESH = pl.DeviceIdType.MESH
block = 128


def packed_rows(size):
    return (size // block // 2) * block


def fold(square):
    top, bottom = square[: block // 2], square[block // 2 :]
    rows = lax.broadcasted_iota(jnp.int32, (block // 2, block), 0)
    columns = lax.broadcasted_iota(jnp.int32, (block // 2, block), 1)
    held = jnp.where(columns > rows + block // 2, pltpu.roll(top, block // 2, 1), bottom)
    return held, jnp.sum(jnp.where(columns == rows, top, 0.0), axis=0, keepdims=True)


def unfold(held, diagonal):
    whole = jnp.concatenate([pltpu.roll(held, block // 2, 1), held], axis=0)
    rows = lax.broadcasted_iota(jnp.int32, (block, block), 0)
    columns = lax.broadcasted_iota(jnp.int32, (block, block), 1)
    is_top = rows < block // 2
    above = is_top & (columns > rows) & (columns < block // 2)
    below = jnp.logical_not(is_top) & (columns <= rows)
    full = jnp.where(above | below, whole, whole.T)
    return jnp.where(is_top & (columns == rows), diagonal, full)


def part_rows(size):
    return -(-(packed_rows(size) + 8) // 16) * 8


def unpack(g_ref, base, turn, full_ref):
    blocks = full_ref.shape[0] // block
    half = blocks // 2
    line = packed_rows(full_ref.shape[0])
    tail = line - block // 2
    notes = [g_ref[turn, base + r, pl.ds(line, 8), :] for r in range(blocks)]

    def put(row, column, value):
        full_ref[pl.ds(row * block, block), pl.ds(column * block, block)] = value

    for r in range(blocks):
        held = g_ref[turn, base + r, pl.ds(0, block // 2), :]
        put(r, r, unfold(held, notes[r][1:2]))
        for d in range(1, half):
            value = g_ref[turn, base + r, pl.ds(d * block - block // 2, block), :]
            put(r, (r + d) % blocks, value)
            put((r + d) % blocks, r, value.T)
    for r in range(half):
        value = jnp.concatenate(
            [g_ref[turn, base + q, pl.ds(tail, block // 2), :] for q in (r, r + half)], axis=0
        )
        put(r, r + half, value)
        put(r + half, r, value.T)
    return jnp.concatenate([note[:1] for note in notes], axis=1)


class Chain:
    def __init__(self, g_ref, frow_ref, qrow_ref, refs, own):
        (
            self.x_all, self.s_rows, self.s_cols, self.y_rows, self.own_y, self.g_full,
            a_ref, ah_ref, xh_ref, e_ref, own_a, own_ah, own_xh, own_e, self.own_x, self.own_row,
            self.ident,
        ) = refs
        self.main, self.side = (a_ref, ah_ref, xh_ref, e_ref), (own_a, own_ah, own_xh, own_e)
        self.g_ref, self.own, self.q_ref = g_ref, own, qrow_ref
        size = frow_ref.shape[1]
        self.blocks = size // block
        self.ident[...] = jnp.where(eye_mask(size), f32(1.0), f32(0.0))
        self.x_all[0] = jnp.zeros((size, size), f32)
        self.s_rows[0] = jnp.zeros((1, size), f32)
        self.s_cols[0] = jnp.zeros((size, 1), f32)
        self.y_rows[0] = jnp.zeros((1, size), f32)
        self.frow = frow_ref[...]
        self.fcol = to_col(self.frow, self.ident)
        self.sq_row = jnp.sqrt(qrow_ref[...])
        self.sq_col = to_col(self.sq_row, self.ident)
        self.f2_row, self.f2_col = self.frow * self.frow, self.fcol * self.fcol
        self.ones = (jnp.ones((1, size), f32), jnp.ones((size, 1), f32))

    def build(self, index, prior, extra):
        prior_row, prior_col = prior
        before = max(index - 1, 0) if isinstance(index, int) else jnp.maximum(index - 1, 0)
        turn = index % self.blocks if isinstance(index, int) else lax.rem(index, self.blocks)
        h = unpack(self.g_ref, index - turn, turn, self.g_full)
        old_row, old_col = self.s_rows[before], self.s_cols[before]
        carried = times_col(self.x_all[before], old_col * to_col(self.y_rows[before], self.ident))
        y = h * self.sq_row + self.frow * (old_row * carried)

        def scaled(row, col, diagonal):
            kept = (self.fcol * old_col * col) * (self.frow * old_row * row)
            added = (self.sq_col * col) * (self.sq_row * row)
            inner = self.g_full[...] * added - self.x_all[before] * kept
            return inner + self.ident[...] * (row * row * diagonal)

        row = lax.rsqrt(prior_row + extra * self.f2_row)
        col = lax.rsqrt(prior_col + extra * self.f2_col)
        a = scaled(row, col, 1.0 + extra * self.f2_row)
        self.main[0][...] = a
        self.main[1][...] = a.astype(bf16)

        @pl.when(index == self.own)
        def _():
            row, col = lax.rsqrt(prior_row), lax.rsqrt(prior_col)
            a = scaled(row, col, f32(1.0))
            self.side[0][...] = a
            self.side[1][...] = a.astype(bf16)
            self.own_row[...] = row
            self.own_y[...] = y

        self.y_rows[index] = y
        self.s_rows[index] = row
        self.s_cols[index] = col

    def next_prior(self, prior):
        return prior[0] / (prior[0] + self.f2_row), prior[1] / (prior[1] + self.f2_col)

    def begin(self, lane):
        return start(lane[0], lane[1], lane[2], self.ident)

    def newton(self, lane, rate):
        return newton(lane[1], lane[2], lane[3], self.ident, rate)

    def finish(self, lane, out_ref):
        return finish(*lane, out_ref, self.ident)

    def filtered(self, mean_ref, var_ref):
        scale = self.own_row[...]
        value = times_col(self.own_x[...], to_col(scale * self.own_y[...], self.ident))
        mean_ref[...] = self.sq_row * scale * value
        diagonal = jnp.sum(self.ident[...] * self.own_x[...], axis=0, keepdims=True)
        var_ref[...] = self.q_ref[...] * scale * scale * diagonal

    def solve_last(self, last):
        a_ref, x_ref = self.main[0], self.main[2]
        last_row = self.s_rows[last]
        goal = last_row * self.y_rows[last]
        x = row_times(x_ref[...], goal)
        for _ in range(2):
            x = x + row_times(x_ref[...], goal - times_col(a_ref[...], x))
        rest = goal - times_col(a_ref[...], x)
        self.y_rows[last] = last_row * jnp.sum(self.ident[...] * x, axis=0, keepdims=True)
        return total(rest * rest) - 2e-7 * total(x * x), goal

    def smooth(self, steps, smooth_ref):
        def back(count, later):
            index = steps - 2 - count
            row = self.s_rows[index]
            value = to_col(row * (self.y_rows[index] + self.frow * later), self.ident)
            return row * times_col(self.x_all[index], value)

        later = lax.fori_loop(0, steps - 1 - self.own, back, self.y_rows[steps - 1])
        smooth_ref[...] = self.sq_row * later


def chain_scratch(steps, size):
    square = pltpu.VMEM((size, size), f32)
    half = pltpu.VMEM((size, size), bf16)
    flat = pltpu.VMEM((1, size), f32)
    return [
        pltpu.VMEM((steps, size, size), f32), pltpu.VMEM((steps, 1, size), f32),
        pltpu.VMEM((steps, size, 1), f32), pltpu.VMEM((steps, 1, size), f32), flat,
        square, square, half, half, half, square, half, half, half, square, flat, square,
    ]


def main_kernel(
    insts, times, quotes_ref, present_ref, noise_ref, loadings_hbm, frow_ref, qrow_ref,
    all_ref, mean_ref, var_ref, smooth_ref, flag_ref, *refs,
):
    (
        loadings_ref, turned_ref, given, rows_ref, pack, landed, load_sem,
        in_send, in_recv, red_send, red_recv, mid_send, out_send, out_recv,
        x_send, x_recv, s_send, s_recv,
    ) = refs[:18]
    size = frow_ref.shape[1]
    blocks = size // block
    part = part_rows(size)
    line = packed_rows(size)
    t, z = lax.axis_index("tm"), lax.axis_index("inst")
    load = pltpu.make_async_copy(loadings_hbm, loadings_ref, load_sem)
    load.start()

    barrier = pltpu.get_barrier_semaphore()
    for k in range(1, insts):
        other = {"inst": lax.rem(z + k, insts)}
        pl.semaphore_signal(barrier, inc=1, device_id=other, device_id_type=MESH)
    for k in range(1, times):
        other = {"tm": lax.rem(t + k, times)}
        pl.semaphore_signal(barrier, inc=1, device_id=other, device_id_type=MESH)

    r, base = lax.rem(t, blocks), t - lax.rem(t, blocks)
    given[r, 0:1, :] = present_ref[...].astype(f32) / noise_ref[...]
    given[r, 1:2, :] = quotes_ref[...]
    drain = []

    def remote(source, target, send, recv, device):
        return pltpu.make_async_remote_copy(
            src_ref=source, dst_ref=target, send_sem=send, recv_sem=recv,
            device_id=device, device_id_type=MESH,
        )

    def same(place, send, recv, device):
        return remote(place, place, send, recv, device)

    def begin(copy, condition=None):
        if condition is None:
            copy.start()
            drain.append(copy.wait_send)
        else:
            pl.when(condition)(copy.start)
            drain.append(lambda: pl.when(condition)(copy.wait_send))

    pl.semaphore_wait(barrier, insts + times - 2)
    for k in range(1, blocks):
        peer = base + lax.rem(r + k, blocks)
        begin(same(given.at[r], in_send.at[k], in_recv.at[k], {"tm": peer}))

    chain = Chain(all_ref, frow_ref, qrow_ref, refs[18:], t)
    load.wait()
    mine = pl.ds(pl.multiple_of(r * block, block), block)
    turned_ref[...] = loadings_ref[:, mine].T
    for k in range(1, blocks):
        source = lax.rem(r + blocks - k, blocks)
        same(given.at[source], in_send.at[k], in_recv.at[k], {"tm": base + source}).wait_recv()

    m1, m2 = insts // 2 - 1, insts // 2
    small = eye_mask(block)

    def weigh(j):
        return (turned_ref[...].astype(f32) * given[j, 0:1, :]).astype(bf16)

    def fill(j, weighted):
        held, diagonal = fold(rows_ref[j, :, mine])
        pack[j, pl.ds(0, block // 2), :] = held
        for d in range(1, blocks // 2):
            column = pl.ds(pl.multiple_of(lax.rem(r + d, blocks) * block, block), block)
            pack[j, pl.ds(d * block - block // 2, block), :] = rows_ref[j, :, column]
        far = pl.ds(pl.multiple_of(lax.rem(r + blocks // 2, blocks) * block, block), block)
        cross = rows_ref[j, :, far]
        upper, lower = cross[: block // 2], cross.T[block // 2 :]
        pack[j, pl.ds(line - block // 2, block // 2), :] = jnp.where(r < blocks // 2, upper, lower)
        sums = jnp.sum(weighted.astype(f32) * given[j, 1:2, :], axis=1, keepdims=True)
        flat = jnp.sum(jnp.where(small, sums, 0.0), axis=0, keepdims=True)
        index = lax.broadcasted_iota(jnp.int32, (2 * part - line, block), 0)
        pack[j, pl.ds(line, 2 * part - line), :] = jnp.where(index == 0, flat, diagonal)

    pairs = times // 2
    spot, core = t // 2, lax.rem(t, 2)
    sibling = {"tm": t + 1 - 2 * core}
    is_right = z >= m2
    near = jnp.where(is_right, 1, 0)
    is_mid = (z == m1) | (z == m2)
    outward, inward = jnp.where(is_right, z + 1, z - 1), jnp.where(is_right, z - 1, z + 1)
    has_outer = (outward >= 0) & (outward < insts)
    not_mid = jnp.logical_not(is_mid)
    outer = {"inst": jnp.clip(outward, 0, insts - 1)}
    inner = {"inst": jnp.clip(inward, 0, insts - 1)}

    def rows_of(half):
        return pl.ds(pl.multiple_of(half * part, 8), part)

    def place(j, source, half):
        return all_ref.at[j, source, rows_of(half)]

    def along_x(k, j, source, half, peer):
        return same(place(j, source, half), x_send.at[k, j, half], x_recv.at[k, j, half], peer)

    def across(k, j, source, half):
        return same(place(j, source, half), s_send.at[k, j, half], s_recv.at[k, j, half], sibling)

    def to_outer(j, half):
        return same(place(j, t, half), out_send.at[j, half], out_recv.at[j, half], outer)

    def to_other(j, half, k):
        peer = {"inst": lax.rem(z + k, insts)}
        return same(place(j, t, half), mid_send.at[j, k], out_recv.at[j, half], peer)

    def to_mid(j, half):
        return same(place(j, t, half), mid_send.at[j, 0], out_recv.at[j, half], inner)

    def inward_part(j, half, slot):
        return remote(
            pack.at[j, rows_of(half)], landed.at[j, slot],
            red_send.at[j, slot], red_recv.at[j, slot], inner,
        )

    def part_to_mid(j, half, source, device):
        return remote(
            pack.at[j, rows_of(half)], landed.at[j, source],
            red_send.at[j, half], red_recv.at[j, source], {"inst": device},
        )

    def send(j):
        if summed[j]:
            outermost = jnp.logical_not(has_outer) & not_mid
            begin(inward_part(j, 1 - near, 0), outermost)
            begin(inward_part(j, near, 1), outermost)
        else:
            for half, mid in enumerate((m1, m2)):
                begin(part_to_mid(j, half, z, mid), z != mid)

    def partial(j):
        if not summed[j]:
            return

        def take(half, slot):
            inward_part(j, half, slot).wait_recv()
            pack[j, rows_of(half), :] += landed[j, slot]

        pl.when(has_outer)(lambda: take(1 - near, 0))
        begin(inward_part(j, 1 - near, 2), is_mid)
        if insts > 4:
            between = has_outer & not_mid
            begin(inward_part(j, 1 - near, 0), between)
            pl.when(between)(lambda: take(near, 1))
            begin(inward_part(j, near, 1), between)

    def near_half(j):
        @pl.when(is_mid)
        def _():
            here = rows_of(near)
            if summed[j]:
                @pl.when(has_outer)
                def _():
                    inward_part(j, near, 1).wait_recv()
                    pack[j, here, :] += landed[j, 1]

                inward_part(j, near, 2).wait_recv()
                all_ref[j, t, here, :] = pack[j, here, :] + landed[j, 2]
            else:
                added = pack[j, here, :]
                for k in range(1, insts):
                    source = lax.rem(z + k, insts)
                    part_to_mid(j, 0, source, source).wait_recv()
                    added = added + landed[j, source]
                all_ref[j, t, here, :] = added

        pl.when(not_mid)(lambda: to_outer(j, near).wait_recv())
        if direct[j]:
            for k in range(1, insts):
                begin(to_other(j, near, k), is_mid)
        else:
            begin(to_mid(j, near), is_mid)
        pass_on(j, near)

    def far_half(j):
        to_outer(j, 1 - near).wait_recv()
        pass_on(j, 1 - near)

    def pass_on(j, half):
        if not direct[j]:
            begin(to_outer(j, half), has_outer)
        for k in range(1, pairs):
            peer = {"tm": lax.rem(spot + k, pairs) * 2 + core}
            begin(along_x(k, j, t, half, peer))
        begin(across(0, j, t, half))

    def from_x(j, half):
        for k in range(1, pairs):
            source = lax.rem(spot + pairs - k, pairs) * 2 + core
            along_x(k, j, source, half, sibling).wait_recv()
            begin(across(k, j, source, half))

    def ready(j):
        for k in range(pairs):
            source = lax.rem(spot + pairs - k, pairs) * 2 + 1 - core
            for half in (near, 1 - near):
                across(k, j, source, half).wait_recv()

    def compute_first():
        weighted = weigh(0)
        rows_ref[0] = mm(weighted, loadings_ref[...])
        fill(0, weighted)

    def compute_others():
        others = [weigh(j) for j in range(1, blocks)]
        products = mm(jnp.concatenate(others, axis=0), loadings_ref[...])
        for j in range(1, blocks):
            rows_ref[j] = products[(j - 1) * block : j * block]
            fill(j, others[j - 1])

    events = {
        "c": lambda j: compute_others() if j else compute_first(), "s": send, "p": partial,
        "n": near_half, "f": far_half, "x": lambda j: from_x(j, near),
        "y": lambda j: from_x(j, 1 - near), "r": ready,
    }

    def run(names):
        for name, turn in zip(names[::2], names[1::2]):
            events[name](int(turn))

    plan = PLAN
    summed, direct = SUMMED, DIRECT
    bad = jnp.zeros((1, 1), f32)
    prior = chain.ones

    def one_step(index, prior, bad, hooks):
        chain.build(index, prior, 1.0)
        _, rate = chain.begin(chain.main)
        run(hooks[0])
        rate = chain.newton(chain.main, rate)
        run(hooks[1])
        rate = chain.newton(chain.main, rate)
        run(hooks[2])
        off = chain.finish(chain.main, chain.x_all.at[index])
        fine = (rate < 0.07) & (off < 0.01)
        return chain.next_prior(prior), jnp.where(fine, bad, 1.0)

    run(plan[0][0])
    for index in range(blocks - 1):
        prior, bad = one_step(index, prior, bad, plan[1 + index])
        run(plan[1 + index][3])
    if times > blocks:

        def later_step(index, carry):
            prior, bad = one_step(index, carry[:2], carry[2], [""] * 3)
            return (*prior, bad)

        *prior, bad = lax.fori_loop(blocks - 1, times - 1, later_step, (*prior, bad))

    last = times - 1
    chain.build(last, prior, 0.0)
    _, rate = chain.begin(chain.main)
    _, own_rate = chain.begin(chain.side)
    for _ in range(3):
        rate = chain.newton(chain.main, rate)
        own_rate = chain.newton(chain.side, own_rate)
    off = chain.finish(chain.side, chain.own_x)
    chain.filtered(mean_ref, var_ref)
    missed, _ = chain.solve_last(last)
    fine = (own_rate < 0.05) & (off < 0.01) & (missed <= 0.0)
    flag_ref[...] = jnp.broadcast_to(jnp.where(fine, bad, 1.0), flag_ref.shape)
    chain.smooth(times, smooth_ref)
    for wait in drain:
        wait()


PLAN = [
    ["c0s0c1s1n0s2n1f0s3x0n2f1x1y0n3r0"],
    ["f2x2", "y1", "f3", "r1"],
    ["x3", "y2", "", "r2"],
    ["y3", "", "", "r3"],
]
SUMMED = [False] * 4
DIRECT = [False] * 4


def smoother(quotes, present, noise_var, loadings, persistence, shock_var, insts, times):
    count, size = loadings.shape
    blocks, part = size // block, part_rows(size)
    whole = pl.BlockSpec(memory_space=pltpu.VMEM)
    dma = pltpu.SemaphoreType.DMA
    pairs = times // 2
    row = jax.ShapeDtypeStruct((1, size), f32)
    return pl.pallas_call(
        functools.partial(main_kernel, insts, times),
        out_shape=(
            jax.ShapeDtypeStruct((blocks, times, 2 * part, block), f32), row, row, row,
            jax.ShapeDtypeStruct((1, block), f32),
        ),
        in_specs=[whole, whole, whole, pl.BlockSpec(memory_space=pl.ANY), whole, whole],
        out_specs=(whole,) * 5,
        scratch_shapes=[
            pltpu.VMEM((count, size), bf16), pltpu.VMEM((block, count), bf16),
            pltpu.VMEM((blocks, 2, count), f32), pltpu.VMEM((blocks, block, size), f32),
            pltpu.VMEM((blocks, 2 * part, block), f32),
            pltpu.VMEM((blocks, max(insts, 3), part, block), f32), dma(()),
            dma((blocks,)), dma((blocks,)), dma((blocks, 3)), dma((blocks, max(insts, 3))),
            dma((blocks, insts)), dma((blocks, 2)), dma((blocks, 2)),
            dma((pairs, blocks, 2)), dma((pairs, blocks, 2)),
            dma((pairs, blocks, 2)), dma((pairs, blocks, 2)),
            *chain_scratch(times, size),
        ],
        compiler_params=pltpu.CompilerParams(
            collective_id=0, has_side_effects=True, vmem_limit_bytes=56 * 1024 * 1024
        ),
    )(quotes, present, noise_var, loadings, persistence, shock_var)


def careful_kernel(
    own_ref, flag_ref, mean_in, var_in, smooth_in, g_hbm, frow_ref, qrow_ref,
    mean_ref, var_ref, smooth_ref, g_ref, work_ref, sem, *refs,
):
    mean_ref[...] = mean_in[...]
    var_ref[...] = var_in[...]
    smooth_ref[...] = smooth_in[...]

    @pl.when(jnp.max(flag_ref[...]) > 0.5)
    def _():
        fetch = pltpu.make_async_copy(g_hbm, g_ref, sem)
        fetch.start()
        fetch.wait()
        chain = Chain(g_ref, frow_ref, qrow_ref, refs, own_ref[0])
        steps, ident_ref = g_ref.shape[1], chain.ident

        def invert(lane, out_ref):
            upper, rate = chain.begin(lane)
            more = more_steps(rate)
            lax.fori_loop(0, more, lambda _, value: chain.newton(lane, value), rate)
            off = jnp.max(chain.finish(lane, out_ref))

            @pl.when(jnp.logical_not(off < 0.002))
            def _():
                careful(lane[0], out_ref, work_ref, ident_ref, upper)

        def step(index, prior):
            chain.build(index, prior, jnp.where(index < steps - 1, 1.0, 0.0))
            invert(chain.main, chain.x_all.at[index])
            return chain.next_prior(prior)

        lax.fori_loop(0, steps, step, chain.ones)
        invert(chain.side, chain.own_x)
        chain.filtered(mean_ref, var_ref)
        last = steps - 1
        row = chain.s_rows[last]
        goal = to_col(row * chain.y_rows[last], ident_ref)
        chain.y_rows[last] = row * times_col(chain.x_all[last], goal)
        chain.smooth(steps, smooth_ref)


def checked(own, flag, rows, matrices, persistence, shock_var):
    steps, size = matrices.shape[1], persistence.shape[1]
    row = jax.ShapeDtypeStruct((1, size), f32)
    whole = pl.BlockSpec(memory_space=pltpu.VMEM)
    return pl.pallas_call(
        careful_kernel,
        out_shape=(row, row, row),
        in_specs=[pl.BlockSpec(memory_space=pltpu.SMEM)] + [whole] * 4
        + [pl.BlockSpec(memory_space=pl.ANY), whole, whole],
        out_specs=(whole, whole, whole),
        scratch_shapes=[
            pltpu.VMEM(matrices.shape, f32), pltpu.VMEM((size, size), f32),
            pltpu.SemaphoreType.DMA(()), *chain_scratch(steps, size),
        ],
        compiler_params=pltpu.CompilerParams(vmem_limit_bytes=60 * 1024 * 1024),
    )(own, flag, *rows, matrices, persistence, shock_var)


def body(quotes, present, loadings, noise_var, persistence, shock_var):
    insts, times = lax.axis_size("inst"), lax.axis_size("tm")
    own = lax.axis_index("tm").astype(jnp.int32)[None]
    persistence, shock_var = persistence[None, :], shock_var[None, :]
    matrices, *rows, flag = smoother(
        quotes, present, noise_var[None, :], loadings, persistence, shock_var, insts, times
    )
    return checked(own, flag, rows, matrices, persistence, shock_var)


def solution(mesh):
    placed = (
        P(("group", "tm"), "inst"),
        P(("group", "tm"), "inst"),
        P("inst", None),
        P("inst"),
        P(),
        P(),
    )
    return jax.shard_map(
        body,
        mesh=mesh,
        in_specs=placed,
        out_specs=(P(("group", "tm"), None), P(("group", "tm"), None), P(("group", "tm"), None)),
        check_vma=False,
    )
```

```python
import functools

import jax
import jax.numpy as jnp
from jax import lax
from jax.experimental import pallas as pl
from jax.experimental.pallas import tpu as pltpu
from jax.sharding import PartitionSpec as P

f32 = jnp.float32
bf16 = jnp.bfloat16
highest = lax.Precision.HIGHEST


def mm(left, right):
    return jnp.dot(left, right, preferred_element_type=f32)


def mm_full(left, right):
    return jnp.dot(left, right, precision=highest, preferred_element_type=f32)


def eye_mask(size):
    rows = lax.broadcasted_iota(jnp.int32, (size, size), 0)
    columns = lax.broadcasted_iota(jnp.int32, (size, size), 1)
    return rows == columns


def total(matrix):
    return jnp.sum(jnp.sum(matrix, axis=0, keepdims=True), axis=1, keepdims=True)


def to_col(row, ident_ref):
    return jnp.sum(ident_ref[...] * row, axis=1, keepdims=True)


def row_times(matrix, row):
    return jnp.sum(matrix.astype(f32) * row, axis=1, keepdims=True)


def times_col(matrix, col):
    return jnp.sum(matrix.astype(f32) * col, axis=0, keepdims=True)


def slower(rate):
    return rate * rate / (2.0 - rate * rate)


def start(a_ref, ah_ref, x_ref, ident_ref):
    square = mm(ah_ref[...], ah_ref[...])
    fourth = total(square * square)
    upper = jnp.maximum(jnp.sqrt(jnp.sqrt(fourth)) * 1.01, 1.5)
    lower = 0.98
    slope = 2.0 / (upper - lower)
    centre = (upper + lower) / (upper - lower)
    height = 1.0 / ((4.0 * centre * centre - 3.0) * centre)
    c0 = (12.0 * centre * centre - 3.0) * slope * height
    c1 = -12.0 * centre * slope * slope * height
    c2 = 4.0 * slope * slope * slope * height
    x_ref[...] = (c0 * ident_ref[...] + c1 * a_ref[...] + c2 * square).astype(bf16)
    return upper, height


def newton(ah_ref, x_ref, e_ref, ident_ref, rate):
    weight = 2.0 / (2.0 - rate * rate)
    e_ref[...] = (ident_ref[...] - mm(ah_ref[...], x_ref[...])).astype(bf16)
    x_ref[...] = (weight * (x_ref[...].astype(f32) + mm(x_ref[...], e_ref[...]))).astype(bf16)
    return slower(rate)


def more_steps(rate):
    count = jnp.zeros_like(rate)
    for _ in range(10):
        count = count + jnp.where(rate > 0.045, 1.0, 0.0)
        rate = slower(rate)
    return jnp.max(count).astype(jnp.int32)


def finish(a_ref, ah_ref, x_ref, e_ref, out_ref, ident_ref):
    low = (a_ref[...] - ah_ref[...].astype(f32)).astype(bf16)
    e = ident_ref[...] - (mm(ah_ref[...], x_ref[...]) + mm(low, x_ref[...]))
    e_ref[...] = e.astype(bf16)
    twice = mm(e_ref[...], e_ref[...])
    e_ref[...] = (e + twice).astype(bf16)
    out_ref[...] = x_ref[...].astype(f32) + mm(x_ref[...], e_ref[...])
    return total(twice * twice)


def careful(a_ref, out_ref, work_ref, ident_ref, upper):
    out_ref[...] = (1.0 / upper) * ident_ref[...]

    def residual():
        e = ident_ref[...] - mm_full(a_ref[...], out_ref[...])
        work_ref[...] = e
        return jnp.sum(e * e)

    def more(state):
        return (state[1] > 1e-6) & (state[0] < 60)

    def refine(state):
        out_ref[...] = out_ref[...] + mm_full(out_ref[...], work_ref[...])
        return (state[0] + 1, residual())

    lax.while_loop(more, refine, (jnp.int32(0), residual()))


MESH = pl.DeviceIdType.MESH
block = 128


def packed_rows(size):
    return (size // block // 2) * block


def fold(square):
    top, bottom = square[: block // 2], square[block // 2 :]
    rows = lax.broadcasted_iota(jnp.int32, (block // 2, block), 0)
    columns = lax.broadcasted_iota(jnp.int32, (block // 2, block), 1)
    held = jnp.where(columns > rows + block // 2, pltpu.roll(top, block // 2, 1), bottom)
    return held, jnp.sum(jnp.where(columns == rows, top, 0.0), axis=0, keepdims=True)


def unfold(held, diagonal):
    whole = jnp.concatenate([pltpu.roll(held, block // 2, 1), held], axis=0)
    rows = lax.broadcasted_iota(jnp.int32, (block, block), 0)
    columns = lax.broadcasted_iota(jnp.int32, (block, block), 1)
    is_top = rows < block // 2
    above = is_top & (columns > rows) & (columns < block // 2)
    below = jnp.logical_not(is_top) & (columns <= rows)
    full = jnp.where(above | below, whole, whole.T)
    return jnp.where(is_top & (columns == rows), diagonal, full)


def part_rows(size):
    return -(-(packed_rows(size) + 8) // 16) * 8


def unpack(g_ref, base, turn, full_ref):
    blocks = full_ref.shape[0] // block
    half = blocks // 2
    line = packed_rows(full_ref.shape[0])
    tail = line - block // 2
    notes = [g_ref[turn, base + r, pl.ds(line, 8), :] for r in range(blocks)]

    def put(row, column, value):
        full_ref[pl.ds(row * block, block), pl.ds(column * block, block)] = value

    for r in range(blocks):
        held = g_ref[turn, base + r, pl.ds(0, block // 2), :]
        put(r, r, unfold(held, notes[r][1:2]))
        for d in range(1, half):
            value = g_ref[turn, base + r, pl.ds(d * block - block // 2, block), :]
            put(r, (r + d) % blocks, value)
            put((r + d) % blocks, r, value.T)
    for r in range(half):
        value = jnp.concatenate(
            [g_ref[turn, base + q, pl.ds(tail, block // 2), :] for q in (r, r + half)], axis=0
        )
        put(r, r + half, value)
        put(r + half, r, value.T)
    return jnp.concatenate([note[:1] for note in notes], axis=1)


class Chain:
    def __init__(self, g_ref, frow_ref, qrow_ref, refs, own):
        (
            self.x_all, self.s_rows, self.s_cols, self.y_rows, self.own_y, self.g_full,
            a_ref, ah_ref, xh_ref, e_ref, own_a, own_ah, own_xh, own_e, self.own_x, self.own_row,
            self.ident,
        ) = refs
        self.main, self.side = (a_ref, ah_ref, xh_ref, e_ref), (own_a, own_ah, own_xh, own_e)
        self.g_ref, self.own, self.q_ref = g_ref, own, qrow_ref
        size = frow_ref.shape[1]
        self.blocks = size // block
        self.ident[...] = jnp.where(eye_mask(size), f32(1.0), f32(0.0))
        self.x_all[0] = jnp.zeros((size, size), f32)
        self.s_rows[0] = jnp.zeros((1, size), f32)
        self.s_cols[0] = jnp.zeros((size, 1), f32)
        self.y_rows[0] = jnp.zeros((1, size), f32)
        self.frow = frow_ref[...]
        self.fcol = to_col(self.frow, self.ident)
        self.sq_row = jnp.sqrt(qrow_ref[...])
        self.sq_col = to_col(self.sq_row, self.ident)
        self.f2_row, self.f2_col = self.frow * self.frow, self.fcol * self.fcol
        self.ones = (jnp.ones((1, size), f32), jnp.ones((size, 1), f32))

    def build(self, index, prior, extra):
        prior_row, prior_col = prior
        before = max(index - 1, 0) if isinstance(index, int) else jnp.maximum(index - 1, 0)
        turn = index % self.blocks if isinstance(index, int) else lax.rem(index, self.blocks)
        h = unpack(self.g_ref, index - turn, turn, self.g_full)
        old_row, old_col = self.s_rows[before], self.s_cols[before]
        carried = times_col(self.x_all[before], old_col * to_col(self.y_rows[before], self.ident))
        y = h * self.sq_row + self.frow * (old_row * carried)

        def scaled(row, col, diagonal):
            kept = (self.fcol * old_col * col) * (self.frow * old_row * row)
            added = (self.sq_col * col) * (self.sq_row * row)
            inner = self.g_full[...] * added - self.x_all[before] * kept
            return inner + self.ident[...] * (row * row * diagonal)

        row = lax.rsqrt(prior_row + extra * self.f2_row)
        col = lax.rsqrt(prior_col + extra * self.f2_col)
        a = scaled(row, col, 1.0 + extra * self.f2_row)
        self.main[0][...] = a
        self.main[1][...] = a.astype(bf16)

        @pl.when(index == self.own)
        def _():
            row, col = lax.rsqrt(prior_row), lax.rsqrt(prior_col)
            a = scaled(row, col, f32(1.0))
            self.side[0][...] = a
            self.side[1][...] = a.astype(bf16)
            self.own_row[...] = row
            self.own_y[...] = y

        self.y_rows[index] = y
        self.s_rows[index] = row
        self.s_cols[index] = col

    def next_prior(self, prior):
        return prior[0] / (prior[0] + self.f2_row), prior[1] / (prior[1] + self.f2_col)

    def begin(self, lane):
        return start(lane[0], lane[1], lane[2], self.ident)

    def newton(self, lane, rate):
        return newton(lane[1], lane[2], lane[3], self.ident, rate)

    def finish(self, lane, out_ref):
        return finish(*lane, out_ref, self.ident)

    def filtered(self, mean_ref, var_ref):
        scale = self.own_row[...]
        value = times_col(self.own_x[...], to_col(scale * self.own_y[...], self.ident))
        mean_ref[...] = self.sq_row * scale * value
        diagonal = jnp.sum(self.ident[...] * self.own_x[...], axis=0, keepdims=True)
        var_ref[...] = self.q_ref[...] * scale * scale * diagonal

    def solve_last(self, last):
        a_ref, x_ref = self.main[0], self.main[2]
        last_row = self.s_rows[last]
        goal = last_row * self.y_rows[last]
        x = row_times(x_ref[...], goal)
        for _ in range(2):
            x = x + row_times(x_ref[...], goal - times_col(a_ref[...], x))
        rest = goal - times_col(a_ref[...], x)
        self.y_rows[last] = last_row * jnp.sum(self.ident[...] * x, axis=0, keepdims=True)
        return total(rest * rest) - 2e-7 * total(x * x), goal

    def smooth(self, steps, smooth_ref):
        def back(count, later):
            index = steps - 2 - count
            row = self.s_rows[index]
            value = to_col(row * (self.y_rows[index] + self.frow * later), self.ident)
            return row * times_col(self.x_all[index], value)

        later = lax.fori_loop(0, steps - 1 - self.own, back, self.y_rows[steps - 1])
        smooth_ref[...] = self.sq_row * later


def chain_scratch(steps, size):
    square = pltpu.VMEM((size, size), f32)
    half = pltpu.VMEM((size, size), bf16)
    flat = pltpu.VMEM((1, size), f32)
    return [
        pltpu.VMEM((steps, size, size), f32), pltpu.VMEM((steps, 1, size), f32),
        pltpu.VMEM((steps, size, 1), f32), pltpu.VMEM((steps, 1, size), f32), flat,
        square, square, half, half, half, square, half, half, half, square, flat, square,
    ]


def main_kernel(
    insts, times, quotes_hbm, present_hbm, noise_hbm, loadings_hbm, frow_hbm, qrow_hbm,
    all_ref, mean_ref, var_ref, smooth_ref, flag_ref, *refs,
):
    (
        loadings_ref, turned_ref, given, rows_ref, pack, landed, load_sem,
        in_send, in_recv, red_send, red_recv, mid_send, out_send, out_recv,
        x_send, x_recv, s_send, s_recv,
        quotes_ref, present_ref, noise_ref, frow_ref, qrow_ref, small_sem,
    ) = refs[:24]
    size = frow_ref.shape[1]
    blocks = size // block
    part = part_rows(size)
    line = packed_rows(size)
    t, z = lax.axis_index("tm"), lax.axis_index("inst")
    barrier = pltpu.get_barrier_semaphore()
    for k in range(1, insts):
        other = {"inst": lax.rem(z + k, insts)}
        pl.semaphore_signal(barrier, inc=1, device_id=other, device_id_type=MESH)
    for k in range(1, times):
        other = {"tm": lax.rem(t + k, times)}
        pl.semaphore_signal(barrier, inc=1, device_id=other, device_id_type=MESH)

    sources = (quotes_hbm, present_hbm, noise_hbm, frow_hbm, qrow_hbm)
    targets = (quotes_ref, present_ref, noise_ref, frow_ref, qrow_ref)
    fetches = [
        pltpu.make_async_copy(source, target, small_sem.at[number])
        for number, (source, target) in enumerate(zip(sources, targets))
    ]
    for fetch in fetches:
        fetch.start()
    load = pltpu.make_async_copy(loadings_hbm, loadings_ref, load_sem)
    load.start()
    for fetch in fetches:
        fetch.wait()
    r, base = lax.rem(t, blocks), t - lax.rem(t, blocks)
    given[r, 0:1, :] = present_ref[...].astype(f32) / noise_ref[...]
    given[r, 1:2, :] = quotes_ref[...]
    drain = []

    def remote(source, target, send, recv, device):
        return pltpu.make_async_remote_copy(
            src_ref=source, dst_ref=target, send_sem=send, recv_sem=recv,
            device_id=device, device_id_type=MESH,
        )

    def same(place, send, recv, device):
        return remote(place, place, send, recv, device)

    def begin(copy, condition=None):
        if condition is None:
            copy.start()
            drain.append(copy.wait_send)
        else:
            pl.when(condition)(copy.start)
            drain.append(lambda: pl.when(condition)(copy.wait_send))

    pl.semaphore_wait(barrier, insts + times - 2)
    for k in range(1, blocks):
        peer = base + lax.rem(r + k, blocks)
        begin(same(given.at[r], in_send.at[k], in_recv.at[k], {"tm": peer}))

    chain = Chain(all_ref, frow_ref, qrow_ref, refs[24:], t)
    load.wait()
    mine = pl.ds(pl.multiple_of(r * block, block), block)
    turned_ref[...] = loadings_ref[:, mine].T
    for k in range(1, blocks):
        source = lax.rem(r + blocks - k, blocks)
        same(given.at[source], in_send.at[k], in_recv.at[k], {"tm": base + source}).wait_recv()

    m1, m2 = insts // 2 - 1, insts // 2
    small = eye_mask(block)

    def weigh(j):
        return (turned_ref[...].astype(f32) * given[j, 0:1, :]).astype(bf16)

    def fill(j, weighted):
        held, diagonal = fold(rows_ref[j, :, mine])
        pack[j, pl.ds(0, block // 2), :] = held
        for d in range(1, blocks // 2):
            column = pl.ds(pl.multiple_of(lax.rem(r + d, blocks) * block, block), block)
            pack[j, pl.ds(d * block - block // 2, block), :] = rows_ref[j, :, column]
        far = pl.ds(pl.multiple_of(lax.rem(r + blocks // 2, blocks) * block, block), block)
        cross = rows_ref[j, :, far]
        upper, lower = cross[: block // 2], cross.T[block // 2 :]
        pack[j, pl.ds(line - block // 2, block // 2), :] = jnp.where(r < blocks // 2, upper, lower)
        sums = jnp.sum(weighted.astype(f32) * given[j, 1:2, :], axis=1, keepdims=True)
        flat = jnp.sum(jnp.where(small, sums, 0.0), axis=0, keepdims=True)
        index = lax.broadcasted_iota(jnp.int32, (2 * part - line, block), 0)
        pack[j, pl.ds(line, 2 * part - line), :] = jnp.where(index == 0, flat, diagonal)

    pairs = times // 2
    spot, core = t // 2, lax.rem(t, 2)
    sibling = {"tm": t + 1 - 2 * core}
    is_right = z >= m2
    near = jnp.where(is_right, 1, 0)
    is_mid = (z == m1) | (z == m2)
    outward, inward = jnp.where(is_right, z + 1, z - 1), jnp.where(is_right, z - 1, z + 1)
    has_outer = (outward >= 0) & (outward < insts)
    not_mid = jnp.logical_not(is_mid)
    outer = {"inst": jnp.clip(outward, 0, insts - 1)}
    inner = {"inst": jnp.clip(inward, 0, insts - 1)}

    def rows_of(half):
        return pl.ds(pl.multiple_of(half * part, 8), part)

    def place(j, source, half):
        return all_ref.at[j, source, rows_of(half)]

    def along_x(k, j, source, half, peer):
        return same(place(j, source, half), x_send.at[k, j, half], x_recv.at[k, j, half], peer)

    def across(k, j, source, half):
        return same(place(j, source, half), s_send.at[k, j, half], s_recv.at[k, j, half], sibling)

    def to_outer(j, half):
        return same(place(j, t, half), out_send.at[j, half], out_recv.at[j, half], outer)

    def to_other(j, half, k):
        peer = {"inst": lax.rem(z + k, insts)}
        return same(place(j, t, half), mid_send.at[j, k], out_recv.at[j, half], peer)

    def to_mid(j, half):
        return same(place(j, t, half), mid_send.at[j, 0], out_recv.at[j, half], inner)

    def inward_part(j, half, slot):
        return remote(
            pack.at[j, rows_of(half)], landed.at[j, slot],
            red_send.at[j, slot], red_recv.at[j, slot], inner,
        )

    def part_to_mid(j, half, source, device):
        return remote(
            pack.at[j, rows_of(half)], landed.at[j, source],
            red_send.at[j, half], red_recv.at[j, source], {"inst": device},
        )

    def send(j):
        if summed[j]:
            outermost = jnp.logical_not(has_outer) & not_mid
            begin(inward_part(j, 1 - near, 0), outermost)
            begin(inward_part(j, near, 1), outermost)
        else:
            for half, mid in enumerate((m1, m2)):
                begin(part_to_mid(j, half, z, mid), z != mid)

    def partial(j):
        if not summed[j]:
            return

        def take(half, slot):
            inward_part(j, half, slot).wait_recv()
            pack[j, rows_of(half), :] += landed[j, slot]

        pl.when(has_outer)(lambda: take(1 - near, 0))
        begin(inward_part(j, 1 - near, 2), is_mid)
        if insts > 4:
            between = has_outer & not_mid
            begin(inward_part(j, 1 - near, 0), between)
            pl.when(between)(lambda: take(near, 1))
            begin(inward_part(j, near, 1), between)

    def near_half(j):
        @pl.when(is_mid)
        def _():
            here = rows_of(near)
            if summed[j]:
                @pl.when(has_outer)
                def _():
                    inward_part(j, near, 1).wait_recv()
                    pack[j, here, :] += landed[j, 1]

                inward_part(j, near, 2).wait_recv()
                all_ref[j, t, here, :] = pack[j, here, :] + landed[j, 2]
            else:
                added = pack[j, here, :]
                for k in range(1, insts):
                    source = lax.rem(z + k, insts)
                    part_to_mid(j, 0, source, source).wait_recv()
                    added = added + landed[j, source]
                all_ref[j, t, here, :] = added

        pl.when(not_mid)(lambda: to_outer(j, near).wait_recv())
        if direct[j]:
            for k in range(1, insts):
                begin(to_other(j, near, k), is_mid)
        else:
            begin(to_mid(j, near), is_mid)
        pass_on(j, near)

    def far_half(j):
        to_outer(j, 1 - near).wait_recv()
        pass_on(j, 1 - near)

    def pass_on(j, half):
        if not direct[j]:
            begin(to_outer(j, half), has_outer)
        for k in range(1, pairs):
            peer = {"tm": lax.rem(spot + k, pairs) * 2 + core}
            begin(along_x(k, j, t, half, peer))
        begin(across(0, j, t, half))

    def from_x(j, half):
        for k in range(1, pairs):
            source = lax.rem(spot + pairs - k, pairs) * 2 + core
            along_x(k, j, source, half, sibling).wait_recv()
            begin(across(k, j, source, half))

    def ready(j):
        for k in range(pairs):
            source = lax.rem(spot + pairs - k, pairs) * 2 + 1 - core
            for half in (near, 1 - near):
                across(k, j, source, half).wait_recv()

    def compute_first():
        weighted = weigh(0)
        rows_ref[0] = mm(weighted, loadings_ref[...])
        fill(0, weighted)

    def compute_others():
        others = [weigh(j) for j in range(1, blocks)]
        products = mm(jnp.concatenate(others, axis=0), loadings_ref[...])
        for j in range(1, blocks):
            rows_ref[j] = products[(j - 1) * block : j * block]
            fill(j, others[j - 1])

    events = {
        "c": lambda j: compute_others() if j else compute_first(), "s": send, "p": partial,
        "n": near_half, "f": far_half, "x": lambda j: from_x(j, near),
        "y": lambda j: from_x(j, 1 - near), "r": ready,
    }

    def run(names):
        for name, turn in zip(names[::2], names[1::2]):
            events[name](int(turn))

    plan = PLAN
    summed, direct = SUMMED, DIRECT
    bad = jnp.zeros((1, 1), f32)
    prior = chain.ones

    def one_step(index, prior, bad, hooks):
        chain.build(index, prior, 1.0)
        _, rate = chain.begin(chain.main)
        run(hooks[0])
        rate = chain.newton(chain.main, rate)
        run(hooks[1])
        rate = chain.newton(chain.main, rate)
        run(hooks[2])
        off = chain.finish(chain.main, chain.x_all.at[index])
        fine = (rate < 0.07) & (off < 0.01)
        return chain.next_prior(prior), jnp.where(fine, bad, 1.0)

    run(plan[0][0])
    for index in range(blocks - 1):
        prior, bad = one_step(index, prior, bad, plan[1 + index])
        run(plan[1 + index][3])
    if times > blocks:

        def later_step(index, carry):
            prior, bad = one_step(index, carry[:2], carry[2], [""] * 3)
            return (*prior, bad)

        *prior, bad = lax.fori_loop(blocks - 1, times - 1, later_step, (*prior, bad))

    last = times - 1
    chain.build(last, prior, 0.0)
    _, rate = chain.begin(chain.main)
    _, own_rate = chain.begin(chain.side)
    for _ in range(3):
        rate = chain.newton(chain.main, rate)
        own_rate = chain.newton(chain.side, own_rate)
    off = chain.finish(chain.side, chain.own_x)
    chain.filtered(mean_ref, var_ref)
    missed, _ = chain.solve_last(last)
    fine = (own_rate < 0.05) & (off < 0.01) & (missed <= 0.0)
    flag_ref[...] = jnp.broadcast_to(jnp.where(fine, bad, 1.0), flag_ref.shape)
    chain.smooth(times, smooth_ref)
    for wait in drain:
        wait()


PLAN = [
    ["c0s0c1s1n0s2n1f0s3x0n2f1x1y0r0"],
    ["n3", "f2", "y1", "x2r1"],
    ["f3", "y2", "", "x3r2"],
    ["", "y3", "", "r3"],
]
SUMMED = [False] * 4
DIRECT = [False] * 4


def smoother(quotes, present, noise_var, loadings, persistence, shock_var, insts, times):
    count, size = loadings.shape
    blocks, part = size // block, part_rows(size)
    whole = pl.BlockSpec(memory_space=pltpu.VMEM)
    dma = pltpu.SemaphoreType.DMA
    pairs = times // 2
    row = jax.ShapeDtypeStruct((1, size), f32)
    return pl.pallas_call(
        functools.partial(main_kernel, insts, times),
        out_shape=(
            jax.ShapeDtypeStruct((blocks, times, 2 * part, block), f32), row, row, row,
            jax.ShapeDtypeStruct((1, block), f32),
        ),
        in_specs=[pl.BlockSpec(memory_space=pl.ANY)] * 6,
        out_specs=(whole,) * 5,
        scratch_shapes=[
            pltpu.VMEM((count, size), bf16), pltpu.VMEM((block, count), bf16),
            pltpu.VMEM((blocks, 2, count), f32), pltpu.VMEM((blocks, block, size), f32),
            pltpu.VMEM((blocks, 2 * part, block), f32),
            pltpu.VMEM((blocks, max(insts, 3), part, block), f32), dma(()),
            dma((blocks,)), dma((blocks,)), dma((blocks, 3)), dma((blocks, max(insts, 3))),
            dma((blocks, insts)), dma((blocks, 2)), dma((blocks, 2)),
            dma((pairs, blocks, 2)), dma((pairs, blocks, 2)),
            dma((pairs, blocks, 2)), dma((pairs, blocks, 2)),
            pltpu.VMEM((1, count), f32), pltpu.VMEM((1, count), jnp.int32),
            pltpu.VMEM((1, count), f32), pltpu.VMEM((1, size), f32), pltpu.VMEM((1, size), f32),
            dma((5,)), *chain_scratch(times, size),
        ],
        compiler_params=pltpu.CompilerParams(
            collective_id=0, has_side_effects=True, vmem_limit_bytes=56 * 1024 * 1024
        ),
    )(quotes, present, noise_var, loadings, persistence, shock_var)


def careful_kernel(
    own_ref, flag_ref, mean_in, var_in, smooth_in, g_hbm, frow_ref, qrow_ref,
    mean_ref, var_ref, smooth_ref, g_ref, work_ref, sem, *refs,
):
    mean_ref[...] = mean_in[...]
    var_ref[...] = var_in[...]
    smooth_ref[...] = smooth_in[...]

    @pl.when(jnp.max(flag_ref[...]) > 0.5)
    def _():
        fetch = pltpu.make_async_copy(g_hbm, g_ref, sem)
        fetch.start()
        fetch.wait()
        chain = Chain(g_ref, frow_ref, qrow_ref, refs, own_ref[0])
        steps, ident_ref = g_ref.shape[1], chain.ident

        def invert(lane, out_ref):
            upper, rate = chain.begin(lane)
            more = more_steps(rate)
            lax.fori_loop(0, more, lambda _, value: chain.newton(lane, value), rate)
            off = jnp.max(chain.finish(lane, out_ref))

            @pl.when(jnp.logical_not(off < 0.002))
            def _():
                careful(lane[0], out_ref, work_ref, ident_ref, upper)

        def step(index, prior):
            chain.build(index, prior, jnp.where(index < steps - 1, 1.0, 0.0))
            invert(chain.main, chain.x_all.at[index])
            return chain.next_prior(prior)

        lax.fori_loop(0, steps, step, chain.ones)
        invert(chain.side, chain.own_x)
        chain.filtered(mean_ref, var_ref)
        last = steps - 1
        row = chain.s_rows[last]
        goal = to_col(row * chain.y_rows[last], ident_ref)
        chain.y_rows[last] = row * times_col(chain.x_all[last], goal)
        chain.smooth(steps, smooth_ref)


def checked(own, flag, rows, matrices, persistence, shock_var):
    steps, size = matrices.shape[1], persistence.shape[1]
    row = jax.ShapeDtypeStruct((1, size), f32)
    whole = pl.BlockSpec(memory_space=pltpu.VMEM)
    return pl.pallas_call(
        careful_kernel,
        out_shape=(row, row, row),
        in_specs=[pl.BlockSpec(memory_space=pltpu.SMEM)] + [whole] * 4
        + [pl.BlockSpec(memory_space=pl.ANY), whole, whole],
        out_specs=(whole, whole, whole),
        scratch_shapes=[
            pltpu.VMEM(matrices.shape, f32), pltpu.VMEM((size, size), f32),
            pltpu.SemaphoreType.DMA(()), *chain_scratch(steps, size),
        ],
        compiler_params=pltpu.CompilerParams(vmem_limit_bytes=60 * 1024 * 1024),
    )(own, flag, *rows, matrices, persistence, shock_var)


def body(quotes, present, loadings, noise_var, persistence, shock_var):
    insts, times = lax.axis_size("inst"), lax.axis_size("tm")
    own = lax.axis_index("tm").astype(jnp.int32)[None]
    persistence, shock_var = persistence[None, :], shock_var[None, :]
    matrices, *rows, flag = smoother(
        quotes, present, noise_var[None, :], loadings, persistence, shock_var, insts, times
    )
    return checked(own, flag, rows, matrices, persistence, shock_var)


def solution(mesh):
    placed = (
        P(("group", "tm"), "inst"),
        P(("group", "tm"), "inst"),
        P("inst", None),
        P("inst"),
        P(),
        P(),
    )
    return jax.shard_map(
        body,
        mesh=mesh,
        in_specs=placed,
        out_specs=(P(("group", "tm"), None), P(("group", "tm"), None), P(("group", "tm"), None)),
        check_vma=False,
    )
```

```python
import functools

import jax
import jax.numpy as jnp
from jax import lax
from jax.experimental import pallas as pl
from jax.experimental.pallas import tpu as pltpu
from jax.sharding import PartitionSpec as P

f32 = jnp.float32
bf16 = jnp.bfloat16
highest = lax.Precision.HIGHEST


def mm(left, right):
    return jnp.dot(left, right, preferred_element_type=f32)


def mm_full(left, right):
    return jnp.dot(left, right, precision=highest, preferred_element_type=f32)


def eye_mask(size):
    rows = lax.broadcasted_iota(jnp.int32, (size, size), 0)
    columns = lax.broadcasted_iota(jnp.int32, (size, size), 1)
    return rows == columns


def total(matrix):
    return jnp.sum(jnp.sum(matrix, axis=0, keepdims=True), axis=1, keepdims=True)


def to_col(row, ident_ref):
    return jnp.sum(ident_ref[...] * row, axis=1, keepdims=True)


def row_times(matrix, row):
    return jnp.sum(matrix.astype(f32) * row, axis=1, keepdims=True)


def times_col(matrix, col):
    return jnp.sum(matrix.astype(f32) * col, axis=0, keepdims=True)


def slower(rate):
    return rate * rate / (2.0 - rate * rate)


def corners(size):
    low, high = pl.ds(0, size // 2), pl.ds(size // 2, size // 2)
    return (low, low), (high, low), (high, high)


def mirror(ref, parts):
    for (rows, columns), value in zip(corners(ref.shape[0]), parts):
        ref[rows, columns] = value
    rows, columns = corners(ref.shape[0])[1]
    ref[columns, rows] = parts[1].T


def start(a_ref, ah_ref, x_ref, ident_ref):
    places = corners(a_ref.shape[0])
    squares = [mm(ah_ref[rows, :], ah_ref[:, columns]) for rows, columns in places]
    first, between, second = squares
    fourth = total(first * first + second * second + 2.0 * (between * between))
    upper = jnp.maximum(jnp.sqrt(jnp.sqrt(fourth)) * 1.01, 1.5)
    lower = 0.98
    slope = 2.0 / (upper - lower)
    centre = (upper + lower) / (upper - lower)
    height = 1.0 / ((4.0 * centre * centre - 3.0) * centre)
    c0 = (12.0 * centre * centre - 3.0) * slope * height
    c1 = -12.0 * centre * slope * slope * height
    c2 = 4.0 * slope * slope * slope * height
    parts = [
        (c0 * ident_ref[place] + c1 * a_ref[place] + c2 * square).astype(bf16)
        for place, square in zip(places, squares)
    ]
    mirror(x_ref, parts)
    return upper, height


def newton(ah_ref, x_ref, e_ref, ident_ref, rate):
    weight = 2.0 / (2.0 - rate * rate)
    places = corners(x_ref.shape[0])
    parts = [
        (ident_ref[rows, columns] - mm(ah_ref[rows, :], x_ref[:, columns])).astype(bf16)
        for rows, columns in places
    ]
    mirror(e_ref, parts)
    parts = [
        (weight * (x_ref[rows, columns].astype(f32) + mm(x_ref[rows, :], e_ref[:, columns])))
        .astype(bf16)
        for rows, columns in places
    ]
    mirror(x_ref, parts)
    return slower(rate)


def finish(a_ref, ah_ref, x_ref, e_ref, out_ref, ident_ref):
    low = (a_ref[...] - ah_ref[...].astype(f32)).astype(bf16)
    e = ident_ref[...] - (mm(ah_ref[...], x_ref[...]) + mm(low, x_ref[...]))
    e_ref[...] = e.astype(bf16)
    twice = mm(e_ref[...], e_ref[...])
    e_ref[...] = (e + twice).astype(bf16)
    out_ref[...] = x_ref[...].astype(f32) + mm(x_ref[...], e_ref[...])
    return total(twice * twice)


def careful(a_ref, out_ref, work_ref, ident_ref):
    sums = jnp.sum(jnp.abs(a_ref[...]), axis=0, keepdims=True)
    out_ref[...] = ident_ref[...] / jnp.max(sums, axis=1, keepdims=True)
    tiles = a_ref.shape[0] // 128

    def residual():
        def tile(number, found):
            rows = pl.ds(pl.multiple_of(number * 128, 128), 128)
            e = ident_ref[rows, :] - mm_full(a_ref[rows, :], out_ref[...])
            work_ref[rows, :] = e
            return found + jnp.sum(e * e)

        return lax.fori_loop(0, tiles, tile, f32(0.0))

    def refine(state):
        def tile(number, carry):
            rows = pl.ds(pl.multiple_of(number * 128, 128), 128)
            out_ref[rows, :] += mm_full(out_ref[rows, :], work_ref[...])
            return carry

        lax.fori_loop(0, tiles, tile, 0)
        return (state[0] + 1, residual())

    def more(state):
        return (state[1] > 1e-6) & (state[0] < 60)

    lax.while_loop(more, refine, (jnp.int32(0), residual()))


MESH = pl.DeviceIdType.MESH
block = 128


def packed_rows(size):
    return (size // block // 2) * block


def fold(square):
    top, bottom = square[: block // 2], square[block // 2 :]
    rows = lax.broadcasted_iota(jnp.int32, (block // 2, block), 0)
    columns = lax.broadcasted_iota(jnp.int32, (block // 2, block), 1)
    held = jnp.where(columns > rows + block // 2, pltpu.roll(top, block // 2, 1), bottom)
    return held, jnp.sum(jnp.where(columns == rows, top, 0.0), axis=0, keepdims=True)


def unfold(held, diagonal):
    whole = jnp.concatenate([pltpu.roll(held, block // 2, 1), held], axis=0)
    rows = lax.broadcasted_iota(jnp.int32, (block, block), 0)
    columns = lax.broadcasted_iota(jnp.int32, (block, block), 1)
    is_top = rows < block // 2
    above = is_top & (columns > rows) & (columns < block // 2)
    below = jnp.logical_not(is_top) & (columns <= rows)
    full = jnp.where(above | below, whole, whole.T)
    return jnp.where(is_top & (columns == rows), diagonal, full)


def part_rows(size):
    return -(-(packed_rows(size) + 8) // 16) * 8


def unpack(g_ref, base, turn, full_ref):
    blocks = full_ref.shape[0] // block
    half = blocks // 2
    line = packed_rows(full_ref.shape[0])
    tail = line - block // 2
    notes = [g_ref[turn, base + r, pl.ds(line, 8), :] for r in range(blocks)]

    def put(row, column, value):
        full_ref[pl.ds(row * block, block), pl.ds(column * block, block)] = value

    for r in range(blocks):
        held = g_ref[turn, base + r, pl.ds(0, block // 2), :]
        put(r, r, unfold(held, notes[r][1:2]))
        for d in range(1, half):
            value = g_ref[turn, base + r, pl.ds(d * block - block // 2, block), :]
            put(r, (r + d) % blocks, value)
            put((r + d) % blocks, r, value.T)
    for r in range(half):
        value = jnp.concatenate(
            [g_ref[turn, base + q, pl.ds(tail, block // 2), :] for q in (r, r + half)], axis=0
        )
        put(r, r + half, value)
        put(r + half, r, value.T)
    return jnp.concatenate([note[:1] for note in notes], axis=1)


class Chain:
    def __init__(self, g_ref, frow_ref, qrow_ref, refs, own):
        (
            self.x_all, self.s_rows, self.s_cols, self.y_rows, self.own_y, self.g_full,
            a_ref, ah_ref, xh_ref, e_ref, own_a, own_ah, own_xh, own_e, self.own_x, self.own_row,
            self.ident,
        ) = refs
        self.main, self.side = (a_ref, ah_ref, xh_ref, e_ref), (own_a, own_ah, own_xh, own_e)
        self.g_ref, self.own, self.q_ref = g_ref, own, qrow_ref
        size = frow_ref.shape[1]
        self.blocks = size // block
        self.ident[...] = jnp.where(eye_mask(size), f32(1.0), f32(0.0))
        self.x_all[0] = jnp.zeros((size, size), f32)
        self.s_rows[0] = jnp.zeros((1, size), f32)
        self.s_cols[0] = jnp.zeros((size, 1), f32)
        self.y_rows[0] = jnp.zeros((1, size), f32)
        self.frow = frow_ref[...]
        self.fcol = to_col(self.frow, self.ident)
        self.sq_row = jnp.sqrt(qrow_ref[...])
        self.sq_col = to_col(self.sq_row, self.ident)
        self.f2_row, self.f2_col = self.frow * self.frow, self.fcol * self.fcol
        self.ones = (jnp.ones((1, size), f32), jnp.ones((size, 1), f32))

    def build(self, index, prior, extra):
        prior_row, prior_col = prior
        before = max(index - 1, 0) if isinstance(index, int) else jnp.maximum(index - 1, 0)
        turn = index % self.blocks if isinstance(index, int) else lax.rem(index, self.blocks)
        h = unpack(self.g_ref, index - turn, turn, self.g_full)
        old_row, old_col = self.s_rows[before], self.s_cols[before]
        carried = times_col(self.x_all[before], old_col * to_col(self.y_rows[before], self.ident))
        y = h * self.sq_row + self.frow * (old_row * carried)

        def scaled(row, col, diagonal):
            kept = (self.fcol * old_col * col) * (self.frow * old_row * row)
            added = (self.sq_col * col) * (self.sq_row * row)
            inner = self.g_full[...] * added - self.x_all[before] * kept
            return inner + self.ident[...] * (row * row * diagonal)

        row = lax.rsqrt(prior_row + extra * self.f2_row)
        col = lax.rsqrt(prior_col + extra * self.f2_col)
        a = scaled(row, col, 1.0 + extra * self.f2_row)
        self.main[0][...] = a
        self.main[1][...] = a.astype(bf16)

        @pl.when(index == self.own)
        def _():
            row, col = lax.rsqrt(prior_row), lax.rsqrt(prior_col)
            a = scaled(row, col, f32(1.0))
            self.side[0][...] = a
            self.side[1][...] = a.astype(bf16)
            self.own_row[...] = row
            self.own_y[...] = y

        self.y_rows[index] = y
        self.s_rows[index] = row
        self.s_cols[index] = col

    def next_prior(self, prior):
        return prior[0] / (prior[0] + self.f2_row), prior[1] / (prior[1] + self.f2_col)

    def begin(self, lane):
        return start(lane[0], lane[1], lane[2], self.ident)

    def newton(self, lane, rate):
        return newton(lane[1], lane[2], lane[3], self.ident, rate)

    def finish(self, lane, out_ref):
        return finish(*lane, out_ref, self.ident)

    def filtered(self, mean_ref, var_ref):
        scale = self.own_row[...]
        value = times_col(self.own_x[...], to_col(scale * self.own_y[...], self.ident))
        mean_ref[...] = self.sq_row * scale * value
        diagonal = jnp.sum(self.ident[...] * self.own_x[...], axis=0, keepdims=True)
        var_ref[...] = self.q_ref[...] * scale * scale * diagonal

    def solve_last(self, last):
        a_ref, x_ref = self.main[0], self.main[2]
        last_row = self.s_rows[last]
        goal = last_row * self.y_rows[last]
        x = row_times(x_ref[...], goal)
        for _ in range(2):
            x = x + row_times(x_ref[...], goal - times_col(a_ref[...], x))
        rest = goal - times_col(a_ref[...], x)
        self.y_rows[last] = last_row * jnp.sum(self.ident[...] * x, axis=0, keepdims=True)
        return total(rest * rest) - 2e-7 * total(x * x), goal

    def smooth(self, steps, smooth_ref):
        def back(count, later):
            index = steps - 2 - count
            row = self.s_rows[index]
            value = to_col(row * (self.y_rows[index] + self.frow * later), self.ident)
            return row * times_col(self.x_all[index], value)

        later = lax.fori_loop(0, steps - 1 - self.own, back, self.y_rows[steps - 1])
        smooth_ref[...] = self.sq_row * later


def chain_scratch(steps, size):
    square = pltpu.VMEM((size, size), f32)
    half = pltpu.VMEM((size, size), bf16)
    flat = pltpu.VMEM((1, size), f32)
    return [
        pltpu.VMEM((steps, size, size), f32), pltpu.VMEM((steps, 1, size), f32),
        pltpu.VMEM((steps, size, 1), f32), pltpu.VMEM((steps, 1, size), f32), flat,
        square, square, half, half, half, square, half, half, half, square, flat, square,
    ]


def main_kernel(
    insts, times, quotes_hbm, present_hbm, noise_hbm, loadings_hbm, frow_hbm, qrow_hbm,
    all_ref, mean_ref, var_ref, smooth_ref, flag_ref, *refs,
):
    (
        loadings_ref, turned_ref, given, rows_ref, pack, landed, load_sem,
        in_send, in_recv, red_send, red_recv, mid_send, out_send, out_recv,
        x_send, x_recv, s_send, s_recv,
        quotes_ref, present_ref, noise_ref, frow_ref, qrow_ref, small_sem,
    ) = refs[:24]
    size = frow_ref.shape[1]
    blocks = size // block
    part = part_rows(size)
    line = packed_rows(size)
    t, z = lax.axis_index("tm"), lax.axis_index("inst")
    barrier = pltpu.get_barrier_semaphore()
    for k in range(1, insts):
        other = {"inst": lax.rem(z + k, insts)}
        pl.semaphore_signal(barrier, inc=1, device_id=other, device_id_type=MESH)
    for k in range(1, times):
        other = {"tm": lax.rem(t + k, times)}
        pl.semaphore_signal(barrier, inc=1, device_id=other, device_id_type=MESH)

    sources = (quotes_hbm, present_hbm, noise_hbm, frow_hbm, qrow_hbm)
    targets = (quotes_ref, present_ref, noise_ref, frow_ref, qrow_ref)
    fetches = [
        pltpu.make_async_copy(source, target, small_sem.at[number])
        for number, (source, target) in enumerate(zip(sources, targets))
    ]
    for fetch in fetches:
        fetch.start()
    load = pltpu.make_async_copy(loadings_hbm, loadings_ref, load_sem)
    load.start()
    for fetch in fetches:
        fetch.wait()
    r, base = lax.rem(t, blocks), t - lax.rem(t, blocks)
    given[r, 0:1, :] = present_ref[...].astype(f32) / noise_ref[...]
    given[r, 1:2, :] = quotes_ref[...]
    drain = []

    def remote(source, target, send, recv, device):
        return pltpu.make_async_remote_copy(
            src_ref=source, dst_ref=target, send_sem=send, recv_sem=recv,
            device_id=device, device_id_type=MESH,
        )

    def same(place, send, recv, device):
        return remote(place, place, send, recv, device)

    def begin(copy, condition=None):
        if condition is None:
            copy.start()
            drain.append(copy.wait_send)
        else:
            pl.when(condition)(copy.start)
            drain.append(lambda: pl.when(condition)(copy.wait_send))

    pl.semaphore_wait(barrier, insts + times - 2)
    for k in range(1, blocks):
        peer = base + lax.rem(r + k, blocks)
        begin(same(given.at[r], in_send.at[k], in_recv.at[k], {"tm": peer}))

    chain = Chain(all_ref, frow_ref, qrow_ref, refs[24:], t)
    load.wait()
    mine = pl.ds(pl.multiple_of(r * block, block), block)
    turned_ref[...] = loadings_ref[:, mine].T
    for k in range(1, blocks):
        source = lax.rem(r + blocks - k, blocks)
        same(given.at[source], in_send.at[k], in_recv.at[k], {"tm": base + source}).wait_recv()

    m1, m2 = insts // 2 - 1, insts // 2
    small = eye_mask(block)

    def weigh(j):
        return (turned_ref[...].astype(f32) * given[j, 0:1, :]).astype(bf16)

    def fill(j, weighted):
        held, diagonal = fold(rows_ref[j, :, mine])
        pack[j, pl.ds(0, block // 2), :] = held
        for d in range(1, blocks // 2):
            column = pl.ds(pl.multiple_of(lax.rem(r + d, blocks) * block, block), block)
            pack[j, pl.ds(d * block - block // 2, block), :] = rows_ref[j, :, column]
        far = pl.ds(pl.multiple_of(lax.rem(r + blocks // 2, blocks) * block, block), block)
        cross = rows_ref[j, :, far]
        upper, lower = cross[: block // 2], cross.T[block // 2 :]
        pack[j, pl.ds(line - block // 2, block // 2), :] = jnp.where(r < blocks // 2, upper, lower)
        sums = jnp.sum(weighted.astype(f32) * given[j, 1:2, :], axis=1, keepdims=True)
        flat = jnp.sum(jnp.where(small, sums, 0.0), axis=0, keepdims=True)
        index = lax.broadcasted_iota(jnp.int32, (2 * part - line, block), 0)
        pack[j, pl.ds(line, 2 * part - line), :] = jnp.where(index == 0, flat, diagonal)

    pairs = times // 2
    spot, core = t // 2, lax.rem(t, 2)
    sibling = {"tm": t + 1 - 2 * core}
    is_right = z >= m2
    near = jnp.where(is_right, 1, 0)
    is_mid = (z == m1) | (z == m2)
    outward, inward = jnp.where(is_right, z + 1, z - 1), jnp.where(is_right, z - 1, z + 1)
    has_outer = (outward >= 0) & (outward < insts)
    not_mid = jnp.logical_not(is_mid)
    outer = {"inst": jnp.clip(outward, 0, insts - 1)}
    inner = {"inst": jnp.clip(inward, 0, insts - 1)}

    def rows_of(half):
        return pl.ds(pl.multiple_of(half * part, 8), part)

    def place(j, source, half):
        return all_ref.at[j, source, rows_of(half)]

    def along_x(k, j, source, half, peer):
        return same(place(j, source, half), x_send.at[k, j, half], x_recv.at[k, j, half], peer)

    def across(k, j, source, half):
        return same(place(j, source, half), s_send.at[k, j, half], s_recv.at[k, j, half], sibling)

    def to_outer(j, half):
        return same(place(j, t, half), out_send.at[j, half], out_recv.at[j, half], outer)

    def to_other(j, half, k):
        peer = {"inst": lax.rem(z + k, insts)}
        return same(place(j, t, half), mid_send.at[j, k], out_recv.at[j, half], peer)

    def to_mid(j, half):
        return same(place(j, t, half), mid_send.at[j, 0], out_recv.at[j, half], inner)

    def inward_part(j, half, slot):
        return remote(
            pack.at[j, rows_of(half)], landed.at[j, slot],
            red_send.at[j, slot], red_recv.at[j, slot], inner,
        )

    def part_to_mid(j, half, source, device):
        return remote(
            pack.at[j, rows_of(half)], landed.at[j, source],
            red_send.at[j, half], red_recv.at[j, source], {"inst": device},
        )

    def send(j):
        if summed[j]:
            outermost = jnp.logical_not(has_outer) & not_mid
            begin(inward_part(j, 1 - near, 0), outermost)
            begin(inward_part(j, near, 1), outermost)
        else:
            for half, mid in enumerate((m1, m2)):
                begin(part_to_mid(j, half, z, mid), z != mid)

    def partial(j):
        if not summed[j]:
            return

        def take(half, slot):
            inward_part(j, half, slot).wait_recv()
            pack[j, rows_of(half), :] += landed[j, slot]

        pl.when(has_outer)(lambda: take(1 - near, 0))
        begin(inward_part(j, 1 - near, 2), is_mid)
        if insts > 4:
            between = has_outer & not_mid
            begin(inward_part(j, 1 - near, 0), between)
            pl.when(between)(lambda: take(near, 1))
            begin(inward_part(j, near, 1), between)

    def near_half(j):
        @pl.when(is_mid)
        def _():
            here = rows_of(near)
            if summed[j]:
                @pl.when(has_outer)
                def _():
                    inward_part(j, near, 1).wait_recv()
                    pack[j, here, :] += landed[j, 1]

                inward_part(j, near, 2).wait_recv()
                all_ref[j, t, here, :] = pack[j, here, :] + landed[j, 2]
            else:
                added = pack[j, here, :]
                for k in range(1, insts):
                    source = lax.rem(z + k, insts)
                    part_to_mid(j, 0, source, source).wait_recv()
                    added = added + landed[j, source]
                all_ref[j, t, here, :] = added

        pl.when(not_mid)(lambda: to_outer(j, near).wait_recv())
        if direct[j]:
            for k in range(1, insts):
                begin(to_other(j, near, k), is_mid)
        else:
            begin(to_mid(j, near), is_mid)
        pass_on(j, near)

    def far_half(j):
        to_outer(j, 1 - near).wait_recv()
        pass_on(j, 1 - near)

    def pass_on(j, half):
        if not direct[j]:
            begin(to_outer(j, half), has_outer)
        for k in range(1, pairs):
            peer = {"tm": lax.rem(spot + k, pairs) * 2 + core}
            begin(along_x(k, j, t, half, peer))
        begin(across(0, j, t, half))

    def from_x(j, half):
        for k in range(1, pairs):
            source = lax.rem(spot + pairs - k, pairs) * 2 + core
            along_x(k, j, source, half, sibling).wait_recv()
            begin(across(k, j, source, half))

    def ready(j):
        for k in range(pairs):
            source = lax.rem(spot + pairs - k, pairs) * 2 + 1 - core
            for half in (near, 1 - near):
                across(k, j, source, half).wait_recv()

    def compute_first():
        weighted = weigh(0)
        rows_ref[0] = mm(weighted, loadings_ref[...])
        fill(0, weighted)

    def compute_others():
        others = [weigh(j) for j in range(1, blocks)]
        products = mm(jnp.concatenate(others, axis=0), loadings_ref[...])
        for j in range(1, blocks):
            rows_ref[j] = products[(j - 1) * block : j * block]
            fill(j, others[j - 1])

    events = {
        "c": lambda j: compute_others() if j else compute_first(), "s": send, "p": partial,
        "n": near_half, "f": far_half, "x": lambda j: from_x(j, near),
        "y": lambda j: from_x(j, 1 - near), "r": ready,
    }

    def run(names):
        for name, turn in zip(names[::2], names[1::2]):
            events[name](int(turn))

    plan = PLAN
    summed, direct = SUMMED, DIRECT
    bad = jnp.zeros((1, 1), f32)
    prior = chain.ones

    def one_step(index, prior, bad, hooks):
        chain.build(index, prior, 1.0)
        _, rate = chain.begin(chain.main)
        run(hooks[0])
        rate = chain.newton(chain.main, rate)
        run(hooks[1])
        rate = chain.newton(chain.main, rate)
        run(hooks[2])
        off = chain.finish(chain.main, chain.x_all.at[index])
        fine = (rate < 0.07) & (off < 0.01)
        return chain.next_prior(prior), jnp.where(fine, bad, 1.0)

    run(plan[0][0])
    for index in range(blocks - 1):
        prior, bad = one_step(index, prior, bad, plan[1 + index])
        run(plan[1 + index][3])
    if times > blocks:

        def later_step(index, carry):
            prior, bad = one_step(index, carry[:2], carry[2], [""] * 3)
            return (*prior, bad)

        *prior, bad = lax.fori_loop(blocks - 1, times - 1, later_step, (*prior, bad))

    last = times - 1
    chain.build(last, prior, 0.0)
    _, rate = chain.begin(chain.main)
    _, own_rate = chain.begin(chain.side)

    def both(_, rates):
        return chain.newton(chain.main, rates[0]), chain.newton(chain.side, rates[1])

    rate, own_rate = lax.fori_loop(0, 3, both, (rate, own_rate))
    off = chain.finish(chain.side, chain.own_x)
    chain.filtered(mean_ref, var_ref)
    missed, _ = chain.solve_last(last)
    fine = (own_rate < 0.05) & (off < 0.01) & (missed <= 0.0)
    flag_ref[...] = jnp.broadcast_to(jnp.where(fine, bad, 1.0), flag_ref.shape)
    chain.smooth(times, smooth_ref)
    for wait in drain:
        wait()


PLAN = [
    ["c0s0c1s1n0s2n1f0s3x0n2f1x1y0r0"],
    ["n3", "f2", "y1", "x2r1"],
    ["f3", "y2", "", "x3r2"],
    ["", "y3", "", "r3"],
]
SUMMED = [False] * 4
DIRECT = [False] * 4


def smoother(quotes, present, noise_var, loadings, persistence, shock_var, insts, times):
    count, size = loadings.shape
    blocks, part = size // block, part_rows(size)
    whole = pl.BlockSpec(memory_space=pltpu.VMEM)
    dma = pltpu.SemaphoreType.DMA
    pairs = times // 2
    row = jax.ShapeDtypeStruct((1, size), f32)
    return pl.pallas_call(
        functools.partial(main_kernel, insts, times),
        out_shape=(
            jax.ShapeDtypeStruct((blocks, times, 2 * part, block), f32), row, row, row,
            jax.ShapeDtypeStruct((1, block), f32),
        ),
        in_specs=[pl.BlockSpec(memory_space=pl.ANY)] * 6,
        out_specs=(whole,) * 5,
        scratch_shapes=[
            pltpu.VMEM((count, size), bf16), pltpu.VMEM((block, count), bf16),
            pltpu.VMEM((blocks, 2, count), f32), pltpu.VMEM((blocks, block, size), f32),
            pltpu.VMEM((blocks, 2 * part, block), f32),
            pltpu.VMEM((blocks, max(insts, 3), part, block), f32), dma(()),
            dma((blocks,)), dma((blocks,)), dma((blocks, 3)), dma((blocks, max(insts, 3))),
            dma((blocks, insts)), dma((blocks, 2)), dma((blocks, 2)),
            dma((pairs, blocks, 2)), dma((pairs, blocks, 2)),
            dma((pairs, blocks, 2)), dma((pairs, blocks, 2)),
            pltpu.VMEM((1, count), f32), pltpu.VMEM((1, count), jnp.int32),
            pltpu.VMEM((1, count), f32), pltpu.VMEM((1, size), f32), pltpu.VMEM((1, size), f32),
            dma((5,)), *chain_scratch(times, size),
        ],
        compiler_params=pltpu.CompilerParams(
            collective_id=0, has_side_effects=True, vmem_limit_bytes=56 * 1024 * 1024
        ),
    )(quotes, present, noise_var, loadings, persistence, shock_var)


def careful_kernel(
    own_ref, flag_ref, mean_in, var_in, smooth_in, g_hbm, frow_ref, qrow_ref,
    mean_ref, var_ref, smooth_ref, g_ref, work_ref, sem, *refs,
):
    mean_ref[...] = mean_in[...]
    var_ref[...] = var_in[...]
    smooth_ref[...] = smooth_in[...]

    @pl.when(jnp.max(flag_ref[...]) > 0.5)
    def _():
        fetch = pltpu.make_async_copy(g_hbm, g_ref, sem)
        fetch.start()
        fetch.wait()
        chain = Chain(g_ref, frow_ref, qrow_ref, refs, own_ref[0])
        steps, ident_ref = g_ref.shape[1], chain.ident

        def step(index, prior):
            @pl.when(index < steps)
            def _():
                chain.build(index, prior, jnp.where(index < steps - 1, 1.0, 0.0))

            @pl.when(index == steps)
            def _():
                chain.main[0][...] = chain.side[0][...]

            careful(chain.main[0], chain.own_x, work_ref, ident_ref)

            @pl.when(index < steps)
            def _():
                chain.x_all[index] = chain.own_x[...]

            return chain.next_prior(prior)

        lax.fori_loop(0, steps + 1, step, chain.ones)
        chain.filtered(mean_ref, var_ref)
        last = steps - 1
        row = chain.s_rows[last]
        goal = to_col(row * chain.y_rows[last], ident_ref)
        chain.y_rows[last] = row * times_col(chain.x_all[last], goal)
        chain.smooth(steps, smooth_ref)


def checked(own, flag, rows, matrices, persistence, shock_var):
    steps, size = matrices.shape[1], persistence.shape[1]
    row = jax.ShapeDtypeStruct((1, size), f32)
    whole = pl.BlockSpec(memory_space=pltpu.VMEM)
    return pl.pallas_call(
        careful_kernel,
        out_shape=(row, row, row),
        in_specs=[pl.BlockSpec(memory_space=pltpu.SMEM)] + [whole] * 4
        + [pl.BlockSpec(memory_space=pl.ANY), whole, whole],
        out_specs=(whole, whole, whole),
        scratch_shapes=[
            pltpu.VMEM(matrices.shape, f32), pltpu.VMEM((size, size), f32),
            pltpu.SemaphoreType.DMA(()), *chain_scratch(steps, size),
        ],
        compiler_params=pltpu.CompilerParams(vmem_limit_bytes=60 * 1024 * 1024),
    )(own, flag, *rows, matrices, persistence, shock_var)


def body(quotes, present, loadings, noise_var, persistence, shock_var):
    insts, times = lax.axis_size("inst"), lax.axis_size("tm")
    own = lax.axis_index("tm").astype(jnp.int32)[None]
    persistence, shock_var = persistence[None, :], shock_var[None, :]
    matrices, *rows, flag = smoother(
        quotes, present, noise_var[None, :], loadings, persistence, shock_var, insts, times
    )
    return checked(own, flag, rows, matrices, persistence, shock_var)


def solution(mesh):
    placed = (
        P(("group", "tm"), "inst"),
        P(("group", "tm"), "inst"),
        P("inst", None),
        P("inst"),
        P(),
        P(),
    )
    return jax.shard_map(
        body,
        mesh=mesh,
        in_specs=placed,
        out_specs=(P(("group", "tm"), None), P(("group", "tm"), None), P(("group", "tm"), None)),
        check_vma=False,
    )
```
